128 devices in a mesh: ctx: 16 (over y_lo, x, core), tp: 8 (over z, y_hi).
Axes of the slice: x: 4, y: 4 (y_hi: 2, y_lo: 2; y = y_hi * 2 + y_lo), z: 4, core: 2. Of those that a mesh axis runs over, the one named last changes fastest.
Arguments:
- se_query: bfloat16 [4096, 8192], P('ctx', 'tp'), may hold values from -6 to 6
- se_key: bfloat16 [4096, 8192], P('ctx', 'tp'), may hold values from -6 to 6
- se_value: bfloat16 [4096, 8192], P('ctx', 'tp'), may hold values from -6 to 6
- se_filter: float32 [512, 7], P('tp'), may hold values from -2.4 to 2.4
- se_skip: float32 [8192], P('tp'), may hold values from -4 to 4
- mr_query: bfloat16 [4096, 8192], P('ctx', 'tp'), may hold values from -6 to 6
- mr_key: bfloat16 [4096, 8192], P('ctx', 'tp'), may hold values from -6 to 6
- mr_value: bfloat16 [4096, 8192], P('ctx', 'tp'), may hold values from -6 to 6
- mr_filter: float32 [512, 128], P('tp'), may hold values from -0.72 to 0.72
- mr_decay: float32 [512], P('tp'), may hold values from 0.005 to 0.1
- mr_skip: float32 [8192], P('tp'), may hold values from -4 to 4
- queries: bfloat16 [4096, 8192], P('ctx', 'tp'), may hold values from -16 to 16
- keys: bfloat16 [4096, 8192], P('ctx', 'tp'), may hold values from -16 to 16
- values: bfloat16 [4096, 8192], P('ctx', 'tp'), may hold values from -6 to 6
- out_weight: bfloat16 [8192, 8192], P('tp'), may hold values from -0.1875 to 0.1875
Outputs:
- se_out: bfloat16 [4096, 8192], P('ctx', 'tp')
- mr_out: bfloat16 [4096, 8192], P('ctx', 'tp')
- attn_out: bfloat16 [4096, 8192], P('ctx', 'tp')
The draws below stay inside these ranges and needn't reach their ends.
All inputs are finite; a program needn't handle non-finite values.
Results may differ from the reference program's by a relative error of at most 0.017.
Values may be sent and summed in bfloat16 or wider, within the bound.
A program may use at most 128 MiB of HBM per device.

```python
import math
import jax
import jax.numpy as jnp
from jax import lax

D = 8192
HEADS = 64
HEAD_DIM = 128
GROUP_WIDTH = 16
SE_TAPS = 7
MR_TAPS = 128
FILTER_GROUPS = 512
SEQ = 4096
N_TP = 8


def drawn_pair(key):
    base = jax.random.fold_in(key, 71)
    first_key, second_key = jax.random.split(base, 2)
    keys_out = jnp.clip(1.6 * jax.random.normal(first_key, (SEQ, D), jnp.float32), -9.6, 9.6)
    queries_out = jnp.clip(1.6 * jax.random.normal(second_key, (SEQ, D), jnp.float32), -9.6, 9.6)
    return (queries_out.astype(jnp.bfloat16), keys_out.astype(jnp.bfloat16))


def draw_queries(key, part):
    return drawn_pair(key)[0]


def draw_keys(key, part):
    return drawn_pair(key)[1]


def block_levels(key, extent, cuts, smallest, largest):
    def one(position, blocks):
        draws = jax.random.uniform(jax.random.fold_in(jax.random.fold_in(key, 6), position), (blocks,), jnp.float32, smallest / len(cuts), largest / len(cuts))
        return jnp.repeat(jnp.exp(draws), extent[position] // blocks).reshape((-1,) + (1,) * (len(extent) - position - 1))

    factor_of = one(*cuts[0])
    for cut in cuts[1:]:
        factor_of = factor_of * one(*cut)
    return factor_of


def gaussian(own_key, extent, width, most, cuts=(), kind=jnp.bfloat16):
    level = block_levels(own_key, extent, cuts, -0.22, 0.18) if cuts else 1.0
    values = jax.random.normal(own_key, extent, jnp.float32) * width * level
    return jnp.minimum(jnp.maximum(values, -most), most).astype(kind)


def setup_inputs(seed: int = 0) -> dict:
    splits = jax.random.split(jax.random.key(seed), 16)
    return {
        "se_query": gaussian(splits[0], (SEQ, D), 1.0, 6.0, ((0, 16), (1, 8))),
        "se_key": gaussian(splits[1], (SEQ, D), 1.0, 6.0, ((0, 16), (1, 8))),
        "se_value": gaussian(splits[2], (SEQ, D), 1.0, 6.0, ((0, 16), (1, 8))),
        "se_filter": gaussian(splits[3], (FILTER_GROUPS, SE_TAPS), 0.4, 2.4, ((0, 8),), jnp.float32),
        "se_skip": gaussian(splits[4], (D,), 1.0, 4.0, ((0, 8),), jnp.float32),
        "mr_query": gaussian(splits[5], (SEQ, D), 1.0, 6.0, ((0, 16), (1, 8))),
        "mr_key": gaussian(splits[6], (SEQ, D), 1.0, 6.0, ((0, 16), (1, 8))),
        "mr_value": gaussian(splits[7], (SEQ, D), 1.0, 6.0, ((0, 16), (1, 8))),
        "mr_filter": gaussian(splits[8], (FILTER_GROUPS, MR_TAPS), 0.12, 0.72, ((0, 8),), jnp.float32),
        "mr_decay": jnp.clip(jnp.exp(math.log(0.1) - 2.9957323 * jax.random.uniform(splits[9], (FILTER_GROUPS,), jnp.float32) ** block_levels(splits[9], (FILTER_GROUPS,), ((0, 8),), -0.2, 0.2)), 0.005, 0.1),
        "mr_skip": gaussian(splits[10], (D,), 1.0, 4.0, ((0, 8),), jnp.float32),
        "queries": draw_queries(jax.random.fold_in(splits[15], 71), 0),
        "keys": draw_keys(jax.random.fold_in(splits[15], 71), 0),
        "values": gaussian(splits[13], (SEQ, D), 1.0, 6.0, ((0, 16), (1, 8))),
        "out_weight": gaussian(splits[14], (D, D), (D // 8) ** -0.5, 0.1875, ((0, 8),)),
    }


def causal_taps(product, channel_taps):
    tap_count = channel_taps.shape[1]
    signal = product.astype(jnp.float32)
    length = signal.shape[0]
    padded = jnp.concatenate([jnp.zeros((tap_count - 1, signal.shape[1]), jnp.float32), signal], axis=0)

    def add_tap(offset_tap, running):
        begin = (tap_count - 1 - offset_tap).astype(jnp.int32)
        shifted = lax.dynamic_slice_in_dim(padded, begin, length, 0)
        column = lax.dynamic_slice_in_dim(channel_taps, jnp.asarray(offset_tap).astype(jnp.int32), 1, 1)
        return running + shifted * column[:, 0][None, :]

    return lax.fori_loop(0, tap_count, add_tap, jnp.zeros_like(signal))


def gated_mixer(query, key_in, value_in, channel_taps, skip):
    product = (key_in.astype(jnp.float32) * value_in.astype(jnp.float32)).astype(jnp.bfloat16)
    convolved = causal_taps(product, channel_taps)
    gated = query.astype(jnp.float32) * (convolved + skip[None, :] * product.astype(jnp.float32))
    return gated.astype(jnp.bfloat16)


def head_attention(operands):
    query_head, key_head, value_head = operands
    length = query_head.shape[0]
    scores = jnp.dot(query_head, key_head.T, preferred_element_type=jnp.float32) * (HEAD_DIM ** -0.5)
    later = jnp.arange(length, dtype=jnp.int32)[:, None] >= jnp.arange(length, dtype=jnp.int32)[None, :]
    row_max = jnp.max(jnp.where(later, scores, -jnp.inf), axis=1)
    expo = jnp.where(later, jnp.exp(scores - row_max[:, None]), jnp.float32(0.0))
    weights = expo.astype(jnp.bfloat16)
    total = jnp.sum(expo, axis=1)
    summed = jnp.dot(weights, value_head, preferred_element_type=jnp.float32)
    return (summed / total[:, None]).astype(jnp.bfloat16)


def reference(se_query, se_key, se_value, se_filter, se_skip, mr_query, mr_key, mr_value, mr_filter, mr_decay, mr_skip, queries, keys, values, out_weight):
    se_channels = jnp.repeat(se_filter, GROUP_WIDTH, axis=0)
    se_out = gated_mixer(se_query, se_key, se_value, se_channels, se_skip)
    tap_index = jnp.arange(MR_TAPS, dtype=jnp.float32)[None, :]
    mr_taps = (mr_filter * jnp.exp(-mr_decay[:, None] * tap_index)).astype(jnp.bfloat16)
    mr_channels = jnp.repeat(mr_taps, GROUP_WIDTH, axis=0).astype(jnp.float32)
    mr_out = gated_mixer(mr_query, mr_key, mr_value, mr_channels, mr_skip)
    length = queries.shape[0]
    split_query = queries.reshape(length, HEADS, HEAD_DIM).transpose(1, 0, 2)
    split_key = keys.reshape(length, HEADS, HEAD_DIM).transpose(1, 0, 2)
    split_value = values.reshape(length, HEADS, HEAD_DIM).transpose(1, 0, 2)
    per_head = lax.map(head_attention, (split_query, split_key, split_value))
    heads = per_head.transpose(1, 0, 2).reshape(length, D)
    block_width = D // N_TP
    projected = jnp.zeros((length, D), jnp.float32)
    for block_index in range(N_TP):
        head_block = heads[:, block_index * block_width:(block_index + 1) * block_width]
        weight_block = out_weight[block_index * block_width:(block_index + 1) * block_width, :]
        partial_sum = jnp.dot(head_block, weight_block, preferred_element_type=jnp.float32).astype(jnp.bfloat16)
        projected = projected + lax.optimization_barrier(partial_sum).astype(jnp.float32)
    attn_out = projected.astype(jnp.bfloat16)
    return (se_out, mr_out, attn_out)
```

```python
import functools
import math

import jax
import jax.numpy as jnp
from jax import lax
from jax.experimental import pallas as pl
from jax.experimental.pallas import tpu as pltpu
from jax.sharding import PartitionSpec as P

F32 = jnp.float32
BF16 = jnp.bfloat16
HEAD = 128
ROWS = 256
CHANS = 1024
TAPS = 128
SHORT = 7
PIECES = 4
PIECE = ROWS // PIECES
EXP_SCALE = HEAD ** (-0.5) * math.log2(math.e)
OFFSETS = ((2, 1), (2, 0), (1, 1), (3, 1), (1, 0), (3, 0), (0, 1))


def kernel(
    sq, sk, sv, sf, ss, mq, mk, mv, mf, md, ms, q, k, v, w,
    se_out, mr_out, attn_out,
    ld, sex, fexp, mrx, rtap, seo, mro, kv, qb, ob, hb, wb, pb,
    far, near, fin, yb, acc_own,
    ld_sem, out_sem, w_sem,
    halo_send, halo_recv,
    kv_send, kv_recv, fwd_send, fwd_recv, q_send, q_recv, h_send, h_recv,
    far_send, far_recv, near_send, near_recv, y_send, y_recv,
):
    c = lax.axis_index("ctx")
    t = lax.axis_index("tp")
    core = lax.rem(c, 2)
    chip = c // 2
    px = lax.rem(chip, 4)
    py = chip // 4
    sib = c + 1 - 2 * core
    z = t // 2
    yh = lax.rem(t, 2)
    zp = lax.rem(z + 1, 4)
    zm = lax.rem(z + 3, 4)
    zf = lax.rem(z + 2, 4)
    up = 2 * zp + yh
    down = 2 * zm + yh
    side = 2 * z + 1 - yh

    def remote(src, dst, send, recv, **where):
        return pltpu.make_async_remote_copy(
            src_ref=src, dst_ref=dst, send_sem=send, recv_sem=recv,
            device_id=where, device_id_type=pl.DeviceIdType.MESH,
        )

    def arrived(dst, send, recv):
        remote(dst, dst, send, recv, ctx=sib).wait_recv()

    loads = [
        pltpu.make_async_copy(src, ld.at[i], ld_sem.at[i])
        for i, src in enumerate((mk, mv, sk, sv, sq, mq))
    ]
    for copy in loads:
        copy.start()

    barrier = pltpu.get_barrier_semaphore()

    def greet(i, _):
        pl.semaphore_signal(
            barrier, inc=1, device_id={"ctx": lax.rem(c + i, 16)},
            device_id_type=pl.DeviceIdType.MESH,
        )
        return 0

    lax.fori_loop(1, 16, greet, 0)
    for peer in (up, down, side):
        pl.semaphore_signal(
            barrier, inc=1, device_id={"tp": peer}, device_id_type=pl.DeviceIdType.MESH
        )

    def product(first, second, r):
        rows = pl.ds(pl.multiple_of(r * 32, 32), 32)
        return (ld[first, rows, :].astype(F32) * ld[second, rows, :].astype(F32)).astype(BF16)

    loads[0].wait()
    loads[1].wait()

    def mr_product(r, _):
        mrx[pl.ds(pl.multiple_of(TAPS + r * 32, 32), 32), :] = product(0, 1, r)
        return 0

    lax.fori_loop(0, ROWS // 32, mr_product, 0)
    loads[2].wait()
    loads[3].wait()

    def se_product(r, _):
        sex[pl.ds(pl.multiple_of(8 + r * 32, 8), 32), :] = product(2, 3, r).astype(F32)
        return 0

    lax.fori_loop(0, ROWS // 32, se_product, 0)

    pl.semaphore_wait(barrier, 18)

    mr_halo = remote(
        mrx.at[pl.ds(ROWS, TAPS)], mrx.at[pl.ds(0, TAPS)],
        halo_send.at[0], halo_recv.at[0], ctx=lax.rem(c + 1, 16),
    )
    se_halo = remote(
        sex.at[pl.ds(ROWS, 8)], sex.at[pl.ds(0, 8)],
        halo_send.at[1], halo_recv.at[1], ctx=lax.rem(c + 1, 16),
    )

    @pl.when(c < 15)
    def _():
        se_halo.start()
        mr_halo.start()

    own_rows = pl.ds(pl.multiple_of(core * ROWS, ROWS), ROWS)
    q_core = lax.rem(core + chip, 2)

    def head_cols(h):
        return pl.ds(pl.multiple_of(h * HEAD, HEAD), HEAD)

    def to_chip(dx, dy):
        return (py + dy - 2 * dy * py) * 4 + lax.rem(px + dx, 4)

    def from_chip(dx, dy):
        return (py + dy - 2 * dy * py) * 4 + lax.rem(px + 4 - dx, 4)

    def kv_copy(i, dest, part):
        return remote(
            (k, v)[part].at[:, head_cols(dest)], kv.at[chip, part, own_rows],
            kv_send.at[i, part], kv_recv.at[chip, part], ctx=2 * dest + core,
        )

    def q_copy(i, dest):
        return remote(
            q.at[:, head_cols(dest)], qb.at[chip],
            q_send.at[i], q_recv.at[chip], ctx=2 * dest + q_core,
        )

    for i, (dx, dy) in enumerate(OFFSETS):
        dest = to_chip(dx, dy)
        kv_copy(i, dest, 0).start()
        kv_copy(i, dest, 1).start()
        q_copy(i, dest).start()
    own_kv = [
        pltpu.make_async_copy(
            src.at[:, head_cols(chip)], kv.at[chip, part, own_rows], kv_recv.at[chip, part]
        )
        for part, src in enumerate((k, v))
    ]
    for copy in own_kv:
        copy.start()
    own_q = pltpu.make_async_copy(q.at[:, head_cols(chip)], qb.at[chip], q_recv.at[chip])
    sib_q = remote(
        q.at[:, head_cols(chip)], qb.at[chip], q_send.at[7], q_recv.at[chip], ctx=sib
    )
    even = lax.rem(chip, 2) == 0

    @pl.when(even)
    def _():
        own_q.start()

    @pl.when(jnp.logical_not(even))
    def _():
        sib_q.start()

    weights = [
        pltpu.make_async_copy(w.at[:, pl.ds(i * CHANS, CHANS)], wb.at[i], w_sem.at[i])
        for i in range(8)
    ]
    for copy in weights:
        copy.start()

    group_of = lax.broadcasted_iota(jnp.int32, (64, CHANS), 1) // 16
    mine = group_of == lax.broadcasted_iota(jnp.int32, (64, CHANS), 0)
    for j in range(SHORT):
        fexp[j : j + 1, :] = jnp.sum(
            jnp.where(mine, sf[:, j : j + 1], 0.0), axis=0, keepdims=True
        )

    @pl.when(c > 0)
    def _():
        arrived(sex.at[pl.ds(0, 8)], halo_send.at[1], halo_recv.at[1])

    @pl.when(c == 0)
    def _():
        sex[0:8, :] = jnp.zeros((8, CHANS), F32)

    loads[4].wait()
    loads[5].wait()

    def short_block(l, _):
        cols = pl.ds(pl.multiple_of(l * 128, 128), 128)
        conv = sex[8 : 8 + ROWS, cols] * fexp[0:1, cols]
        for j in range(1, SHORT):
            conv = conv + sex[8 - j : 8 - j + ROWS, cols] * fexp[j : j + 1, cols]
        skipped = ss[0:1, cols] * sex[8 : 8 + ROWS, cols]
        seo[:, cols] = (ld[4, :, cols].astype(F32) * (conv + skipped)).astype(BF16)
        return 0

    lax.fori_loop(0, 8, short_block, 0)
    put_se = pltpu.make_async_copy(seo, se_out, out_sem.at[0])
    put_se.start()

    row64 = lax.broadcasted_iota(jnp.int32, (64, 64), 0)
    lane64 = lax.broadcasted_iota(jnp.int32, (64, 64), 1)
    decay = jnp.sum(jnp.where(row64 == lane64, md[...], 0.0), axis=1, keepdims=True)
    tap_index = lax.broadcasted_iota(jnp.int32, (64, TAPS), 1).astype(F32)
    taps = (mf[...] * jnp.exp(-decay * tap_index)).astype(BF16)
    r128 = lax.broadcasted_iota(jnp.int32, (TAPS, TAPS), 0)
    l128 = lax.broadcasted_iota(jnp.int32, (TAPS, TAPS), 1)
    flip = jnp.where(lax.rem(r128 + l128, TAPS) == 0, 1.0, 0.0).astype(BF16)
    rtap[...] = jnp.dot(taps, flip, preferred_element_type=F32)

    @pl.when(c > 0)
    def _():
        arrived(mrx.at[pl.ds(0, TAPS)], halo_send.at[0], halo_recv.at[0])

    @pl.when(c == 0)
    def _():
        mrx[0:TAPS, :] = jnp.zeros((TAPS, CHANS), BF16)

    later = l128 > r128
    lane_group = lax.rem(lax.broadcasted_iota(jnp.int32, (TAPS, 2 * TAPS), 1), TAPS) // 16

    def medium_block(l, _):
        cols = pl.ds(pl.multiple_of(l * 128, 128), 128)
        window = jnp.concatenate(
            [mrx[0 : 2 * TAPS, cols], mrx[TAPS : 3 * TAPS, cols]], axis=1
        )
        block_taps = rtap[pl.ds(pl.multiple_of(l * 8, 8), 8), :]
        conv = jnp.zeros((TAPS, 2 * TAPS), F32)
        for g in range(8):
            row = jnp.broadcast_to(block_taps[g : g + 1, :], (TAPS, TAPS))
            turned = pltpu.roll(row, 0, 1, stride=1, stride_axis=0)
            table = jnp.concatenate(
                [jnp.where(later, turned, 0.0), jnp.where(later, 0.0, turned)], axis=1
            ).astype(BF16)
            conv = jnp.where(
                lane_group == g, jnp.dot(table, window, preferred_element_type=F32), conv
            )
        for b in range(2):
            rows = pl.ds(b * TAPS, TAPS)
            source = mrx[TAPS + b * TAPS : 2 * TAPS + b * TAPS, cols].astype(F32)
            total = conv[:, b * TAPS : (b + 1) * TAPS] + ms[0:1, cols] * source
            mro[rows, cols] = (ld[5, rows, cols].astype(F32) * total).astype(BF16)
        return 0

    lax.fori_loop(0, 8, medium_block, 0)
    put_mr = pltpu.make_async_copy(mro, mr_out, out_sem.at[1])
    put_mr.start()

    def forward(src_chip):
        piece = kv.at[src_chip, :, own_rows]
        return remote(
            piece, piece, fwd_send.at[src_chip], fwd_recv.at[src_chip], ctx=sib
        )

    sources = [chip] + [from_chip(dx, dy) for dx, dy in OFFSETS]
    for src_chip in sources:
        for part in range(2):
            arrived(
                kv.at[src_chip, part, own_rows], fwd_send.at[src_chip], kv_recv.at[src_chip, part]
            )
        forward(src_chip).start()
    sib_rows = pl.ds(pl.multiple_of((1 - core) * ROWS, ROWS), ROWS)

    def all_here(i, _):
        arrived(kv.at[i, :, sib_rows], fwd_send.at[i], fwd_recv.at[i])
        arrived(qb.at[i], q_send.at[0], q_recv.at[i])
        return 0

    lax.fori_loop(0, 8, all_here, 0)

    def scores_of(query, chunk):
        return lax.dot_general(
            query, kv[chunk, 0], (((1,), (1,)), ((), ())), preferred_element_type=F32
        )

    def lane_sum(x):
        return x[:, 0:128] + x[:, 128:256] + x[:, 256:384] + x[:, 384:512]

    q_row = lax.broadcasted_iota(jnp.int32, (ROWS, 2 * ROWS), 0)
    k_row = lax.broadcasted_iota(jnp.int32, (ROWS, 2 * ROWS), 1)

    def head_copy(slot):
        half = lax.rem(core + slot, 2)
        return remote(
            ob.at[slot], hb.at[:, head_cols(chip)],
            h_send.at[slot], h_recv.at[chip], ctx=2 * slot + half,
        )

    def attend(o, _):
        slot = lax.rem(chip + 1 + o, 8)
        half = lax.rem(core + slot, 2)
        query = qb[slot]
        s = jnp.where(k_row <= q_row + half * ROWS, scores_of(query, slot), -1e30)
        top = jnp.max(s, axis=1, keepdims=True)
        expo = jnp.exp2((s - top) * EXP_SCALE)
        norm = lane_sum(expo)
        mixed = jnp.dot(expo.astype(BF16), kv[slot, 1], preferred_element_type=F32)

        def step(chunk, carry):
            top, norm, mixed = carry
            s = scores_of(query, chunk)
            new_top = jnp.maximum(top, jnp.max(s, axis=1, keepdims=True))
            factor = jnp.exp2((top - new_top) * EXP_SCALE)
            expo = jnp.exp2((s - new_top) * EXP_SCALE)
            norm = norm * factor + lane_sum(expo)
            mixed = mixed * factor + jnp.dot(
                expo.astype(BF16), kv[chunk, 1], preferred_element_type=F32
            )
            return new_top, norm, mixed

        top, norm, mixed = lax.fori_loop(0, slot, step, (top, norm, mixed))
        ob[slot] = (mixed / jnp.sum(norm, axis=1, keepdims=True)).astype(BF16)
        stays = jnp.logical_and(slot == chip, even)

        @pl.when(stays)
        def _():
            pltpu.make_async_copy(ob.at[slot], hb.at[:, head_cols(chip)], h_recv.at[chip]).start()

        @pl.when(jnp.logical_not(stays))
        def _():
            head_copy(slot).start()

        return 0

    lax.fori_loop(0, 8, attend, 0)

    def heads_here(i, _):
        arrived(hb.at[:, head_cols(i)], h_send.at[0], h_recv.at[i])
        return 0

    lax.fori_loop(0, 8, heads_here, 0)
    for copy in weights:
        copy.wait()

    def project(block):
        def columns(n, _):
            cols = pl.ds(pl.multiple_of(n * 256, 256), 256)
            pb[block, :, cols] = jnp.dot(
                hb[...], wb[block, :, cols], preferred_element_type=F32
            ).astype(BF16)
            return 0

        lax.fori_loop(0, CHANS // 256, columns, 0)

    def piece(r):
        return pl.ds(r * PIECE, PIECE)

    ahead = (zp, zm)
    to = (up, down)

    def far_copy(d, r):
        return remote(
            pb.at[2 * zf + d, piece(r)], far.at[d, piece(r)],
            far_send.at[d, r], far_recv.at[d, r], tp=to[d],
        )

    def near_copy(d, h, r):
        return remote(
            pb.at[2 * ahead[d] + h, piece(r)], near.at[d, h, piece(r)],
            near_send.at[d, h, r], near_recv.at[d, h, r], tp=to[d],
        )

    def side_copy(r):
        return remote(
            fin.at[piece(r)], yb.at[piece(r)], y_send.at[r], y_recv.at[r], tp=side
        )

    def finish(r):
        for d in range(2):
            for h in range(2):
                near_copy(d, h, r).wait_recv()

        def total(h):
            return (
                pb[2 * z + h, piece(r), :].astype(F32)
                + near[0, h, piece(r), :].astype(F32)
                + near[1, h, piece(r), :].astype(F32)
            )

        fin[piece(r), :] = total(1 - yh).astype(BF16)
        side_copy(r).start()
        acc_own[piece(r), :] = total(yh)

    project(2 * zf)
    project(2 * zf + 1)
    for d in range(2):
        far_copy(d, 0).start()
    project(2 * zp + 1)
    project(2 * zm)
    for d in range(2):
        near_copy(d, 1 - d, 0).start()
        far_copy(d, 1).start()
    project(2 * zp)
    project(2 * zm + 1)
    for r in range(PIECES):
        for d in range(2):
            far_copy(d, r).wait_recv()
            block = 2 * ahead[d] + d
            pb[block, piece(r), :] = (
                pb[block, piece(r), :].astype(F32) + far[d, piece(r), :].astype(F32)
            ).astype(BF16)
            near_copy(d, d, r).start()
        for d in range(2):
            if r + 1 < PIECES:
                near_copy(d, 1 - d, r + 1).start()
            if r + 2 < PIECES:
                far_copy(d, r + 2).start()
        if r == 0:
            project(2 * z)
            project(2 * z + 1)
        else:
            finish(r - 1)
    finish(PIECES - 1)
    for r in range(PIECES):
        side_copy(r).wait_recv()
        seo_rows = piece(r)
        ob_out = (acc_own[seo_rows, :] + yb[seo_rows, :].astype(F32)).astype(BF16)
        fin_out = ld.at[0]
        fin_out[seo_rows, :] = ob_out
    put_attn = pltpu.make_async_copy(ld.at[0], attn_out, out_sem.at[2])
    put_attn.start()

    @pl.when(c < 15)
    def _():
        se_halo.wait_send()
        mr_halo.wait_send()

    for i, (dx, dy) in enumerate(OFFSETS):
        dest = to_chip(dx, dy)
        kv_copy(i, dest, 0).wait_send()
        kv_copy(i, dest, 1).wait_send()
        q_copy(i, dest).wait_send()

    @pl.when(jnp.logical_not(even))
    def _():
        sib_q.wait_send()

    def forwarded(i, _):
        forward(i).wait_send()
        stays = jnp.logical_and(i == chip, even)

        @pl.when(jnp.logical_not(stays))
        def _():
            head_copy(i).wait_send()

        return 0

    lax.fori_loop(0, 8, forwarded, 0)
    for r in range(PIECES):
        side_copy(r).wait_send()
        for d in range(2):
            far_copy(d, r).wait_send()
            for h in range(2):
                near_copy(d, h, r).wait_send()
    put_se.wait()
    put_mr.wait()
    put_attn.wait()


def local(*args):
    (sq, sk, sv, sf, ss, mq, mk, mv, mf, md, ms, q, k, v, w) = args
    any_spec = pl.BlockSpec(memory_space=pl.ANY)
    vmem = pl.BlockSpec(memory_space=pltpu.VMEM)
    out = jax.ShapeDtypeStruct((ROWS, CHANS), BF16)
    dma = pltpu.SemaphoreType.DMA
    return pl.pallas_call(
        kernel,
        name="mixers",
        out_shape=(out, out, out),
        in_specs=[any_spec] * 3 + [vmem] * 2 + [any_spec] * 3 + [vmem] * 3 + [any_spec] * 4,
        out_specs=(any_spec,) * 3,
        scratch_shapes=[
            pltpu.VMEM((6, ROWS, CHANS), BF16),
            pltpu.VMEM((8 + ROWS, CHANS), F32),
            pltpu.VMEM((8, CHANS), F32),
            pltpu.VMEM((TAPS + ROWS, CHANS), BF16),
            pltpu.VMEM((64, TAPS), F32),
            pltpu.VMEM((ROWS, CHANS), BF16),
            pltpu.VMEM((ROWS, CHANS), BF16),
            pltpu.VMEM((8, 2, 2 * ROWS, HEAD), BF16),
            pltpu.VMEM((8, ROWS, HEAD), BF16),
            pltpu.VMEM((8, ROWS, HEAD), BF16),
            pltpu.VMEM((ROWS, CHANS), BF16),
            pltpu.VMEM((8, CHANS, CHANS), BF16),
            pltpu.VMEM((8, ROWS, CHANS), BF16),
            pltpu.VMEM((2, ROWS, CHANS), BF16),
            pltpu.VMEM((2, 2, ROWS, CHANS), BF16),
            pltpu.VMEM((ROWS, CHANS), BF16),
            pltpu.VMEM((ROWS, CHANS), BF16),
            pltpu.VMEM((ROWS, CHANS), F32),
            dma((6,)), dma((3,)), dma((8,)),
            dma((2,)), dma((2,)),
            dma((7, 2)), dma((8, 2)), dma((8,)), dma((8,)),
            dma((8,)), dma((8,)), dma((8,)), dma((8,)),
            dma((2, PIECES)), dma((2, PIECES)),
            dma((2, 2, PIECES)), dma((2, 2, PIECES)),
            dma((PIECES,)), dma((PIECES,)),
        ],
        compiler_params=pltpu.CompilerParams(
            collective_id=0, has_side_effects=True, vmem_limit_bytes=56 * 1024 * 1024
        ),
        cost_estimate=pl.CostEstimate(
            flops=12 * 10**9, bytes_accessed=28 * 2**20, transcendentals=5 * 10**6
        ),
    )(
        sq, sk, sv, sf, ss.reshape(1, CHANS), mq, mk, mv, mf, md.reshape(1, 64),
        ms.reshape(1, CHANS), q, k, v, w,
    )


def solution(mesh):
    block = P("ctx", "tp")
    in_specs = (
        block, block, block, P("tp", None), P("tp"),
        block, block, block, P("tp", None), P("tp"), P("tp"),
        block, block, block, P("tp", None),
    )
    return jax.shard_map(
        local, mesh=mesh, in_specs=in_specs, out_specs=(block, block, block), check_vma=False
    )
```

```python
import functools
import math

import jax
import jax.numpy as jnp
from jax import lax
from jax.experimental import pallas as pl
from jax.experimental.pallas import tpu as pltpu
from jax.sharding import PartitionSpec as P

F32 = jnp.float32
BF16 = jnp.bfloat16
HEAD = 128
ROWS = 256
CHANS = 1024
TAPS = 128
SHORT = 7
PIECE = 32
HALF = PIECE // 2
Z_FIRST = 4
Y_FIRST = ROWS // PIECE - Z_FIRST
F_ROWS = Z_FIRST * PIECE
G_ROWS = Y_FIRST * PIECE
EXP_SCALE = HEAD ** (-0.5) * math.log2(math.e)
OFFSETS = ((0, 0), (1, 0), (0, 1), (3, 0), (1, 1), (2, 0), (3, 1), (2, 1))


def kernel(
    sq, sk, sv, sf, ss, mq, mk, mv, mf, md, ms, q, k, v, w,
    se_out, mr_out, attn_out,
    ld, sex, fexp, mrx, rtap, seo, mro, kv, qb, ob, hb, wb, pb, tops, norms, mixes,
    far, near, fin, yb, acc_own, gy, gfar, gnear,
    ld_sem, out_sem, w_sem,
    halo_send, halo_recv,
    kv_send, kv_recv, fwd_send, fwd_recv, q_send, q_recv, h_send, h_recv,
    far_send, far_recv, near_send, near_recv, y_send, y_recv,
    gy_send, gy_recv, gfar_send, gfar_recv, gnear_send, gnear_recv,
):
    c = lax.axis_index("ctx")
    t = lax.axis_index("tp")
    core = lax.rem(c, 2)
    chip = c // 2
    px = lax.rem(chip, 4)
    py = chip // 4
    sib = c + 1 - 2 * core
    z = t // 2
    yh = lax.rem(t, 2)
    zp = lax.rem(z + 1, 4)
    zm = lax.rem(z + 3, 4)
    zf = lax.rem(z + 2, 4)
    up = 2 * zp + yh
    down = 2 * zm + yh
    side = 2 * z + 1 - yh

    def remote(src, dst, send, recv, **where):
        return pltpu.make_async_remote_copy(
            src_ref=src, dst_ref=dst, send_sem=send, recv_sem=recv,
            device_id=where, device_id_type=pl.DeviceIdType.MESH,
        )

    def arrived(dst, send, recv):
        remote(dst, dst, send, recv, ctx=sib).wait_recv()

    loads = [
        pltpu.make_async_copy(src, ld.at[i], ld_sem.at[i])
        for i, src in enumerate((mk, mv, sk, sv, sq, mq))
    ]
    for copy in loads:
        copy.start()

    barrier = pltpu.get_barrier_semaphore()

    def greet(i, _):
        pl.semaphore_signal(
            barrier, inc=1, device_id={"ctx": lax.rem(c + i, 16)},
            device_id_type=pl.DeviceIdType.MESH,
        )
        return 0

    lax.fori_loop(1, 16, greet, 0)
    for peer in (up, down, side):
        pl.semaphore_signal(
            barrier, inc=1, device_id={"tp": peer}, device_id_type=pl.DeviceIdType.MESH
        )

    pl.semaphore_wait(barrier, 18)

    own_rows = pl.ds(pl.multiple_of(core * ROWS, ROWS), ROWS)
    q_core = lax.rem(core + chip, 2)

    def head_cols(h):
        return pl.ds(pl.multiple_of(h * HEAD, HEAD), HEAD)

    def to_chip(dx, dy):
        return (py + dy - 2 * dy * py) * 4 + lax.rem(px + dx, 4)

    def source(n):
        dx = sum(jnp.where(n == i, d[0], 0) for i, d in enumerate(OFFSETS))
        dy = sum(jnp.where(n == i, d[1], 0) for i, d in enumerate(OFFSETS))
        return (py + dy - 2 * dy * py) * 4 + lax.rem(px + 4 - dx, 4)

    def kv_copy(i, dest, part):
        return remote(
            (k, v)[part].at[:, head_cols(dest)], kv.at[chip, part, own_rows],
            kv_send.at[i, part], kv_recv.at[chip, part], ctx=2 * dest + core,
        )

    def q_copy(i, dest):
        return remote(
            q.at[:, head_cols(dest)], qb.at[chip],
            q_send.at[i], q_recv.at[chip], ctx=2 * dest + q_core,
        )

    for i, (dx, dy) in enumerate(OFFSETS[1:]):
        q_copy(i, to_chip(dx, dy)).start()
    def send_kv(first, last):
        for i in range(first, last):
            dest = to_chip(*OFFSETS[i + 1])
            kv_copy(i, dest, 0).start()
            kv_copy(i, dest, 1).start()

    send_kv(0, 3)
    own_kv = [
        pltpu.make_async_copy(
            src.at[:, head_cols(chip)], kv.at[chip, part, own_rows], kv_recv.at[chip, part]
        )
        for part, src in enumerate((k, v))
    ]
    for copy in own_kv:
        copy.start()
    own_q = pltpu.make_async_copy(q.at[:, head_cols(chip)], qb.at[chip], q_recv.at[chip])
    sib_q = remote(
        q.at[:, head_cols(chip)], qb.at[chip], q_send.at[7], q_recv.at[chip], ctx=sib
    )
    even = lax.rem(chip, 2) == 0

    @pl.when(even)
    def _():
        own_q.start()

    @pl.when(jnp.logical_not(even))
    def _():
        sib_q.start()

    def product(first, second, r):
        rows = pl.ds(pl.multiple_of(r * 32, 32), 32)
        return (ld[first, rows, :].astype(F32) * ld[second, rows, :].astype(F32)).astype(BF16)

    loads[0].wait()
    loads[1].wait()

    def mr_product(r, _):
        mrx[pl.ds(pl.multiple_of(TAPS + r * 32, 32), 32), :] = product(0, 1, r)
        return 0

    lax.fori_loop(0, ROWS // 32, mr_product, 0)
    loads[2].wait()
    loads[3].wait()

    def se_product(r, _):
        sex[pl.ds(pl.multiple_of(8 + r * 32, 8), 32), :] = product(2, 3, r).astype(F32)
        return 0

    lax.fori_loop(0, ROWS // 32, se_product, 0)

    mr_halo = remote(
        mrx.at[pl.ds(ROWS, TAPS)], mrx.at[pl.ds(0, TAPS)],
        halo_send.at[0], halo_recv.at[0], ctx=lax.rem(c + 1, 16),
    )
    se_halo = remote(
        sex.at[pl.ds(ROWS, 8)], sex.at[pl.ds(0, 8)],
        halo_send.at[1], halo_recv.at[1], ctx=lax.rem(c + 1, 16),
    )

    @pl.when(c < 15)
    def _():
        se_halo.start()
        mr_halo.start()

    send_kv(3, 7)
    weights = [
        pltpu.make_async_copy(w.at[:, pl.ds(i * CHANS, CHANS)], wb.at[i], w_sem.at[i])
        for i in range(8)
    ]
    for copy in weights:
        copy.start()

    group_of = lax.broadcasted_iota(jnp.int32, (64, CHANS), 1) // 16
    mine = group_of == lax.broadcasted_iota(jnp.int32, (64, CHANS), 0)
    row64 = lax.broadcasted_iota(jnp.int32, (64, 64), 0)
    lane64 = lax.broadcasted_iota(jnp.int32, (64, 64), 1)

    def as_column(row):
        return jnp.sum(jnp.where(row64 == lane64, row, 0.0), axis=1, keepdims=True)

    for j in range(SHORT):
        fexp[j : j + 1, :] = jnp.sum(
            jnp.where(mine, as_column(sf[j : j + 1, :]), 0.0), axis=0, keepdims=True
        )

    def short_block(l, _):
        cols = pl.ds(pl.multiple_of(l * 128, 128), 128)
        conv = sex[8 : 8 + ROWS, cols] * fexp[0:1, cols]
        for j in range(1, SHORT):
            conv = conv + sex[8 - j : 8 - j + ROWS, cols] * fexp[j : j + 1, cols]
        skipped = ss[0:1, cols] * sex[8 : 8 + ROWS, cols]
        seo[:, cols] = (ld[4, :, cols].astype(F32) * (conv + skipped)).astype(BF16)
        return 0

    decay = as_column(md[...])
    tap_index = lax.broadcasted_iota(jnp.int32, (64, TAPS), 1).astype(F32)
    taps = (mf[...] * jnp.exp(-decay * tap_index)).astype(BF16)
    r128 = lax.broadcasted_iota(jnp.int32, (TAPS, TAPS), 0)
    l128 = lax.broadcasted_iota(jnp.int32, (TAPS, TAPS), 1)
    flip = jnp.where(lax.rem(r128 + l128, TAPS) == 0, 1.0, 0.0).astype(BF16)
    rtap[...] = jnp.dot(taps, flip, preferred_element_type=F32)

    later = l128 > r128
    lane_group = lax.rem(lax.broadcasted_iota(jnp.int32, (TAPS, 2 * TAPS), 1), TAPS) // 16

    def medium_block(l, _):
        cols = pl.ds(pl.multiple_of(l * 128, 128), 128)
        window = jnp.concatenate(
            [mrx[0 : 2 * TAPS, cols], mrx[TAPS : 3 * TAPS, cols]], axis=1
        )
        block_taps = rtap[pl.ds(pl.multiple_of(l * 8, 8), 8), :]
        conv = jnp.zeros((TAPS, 2 * TAPS), F32)
        for g in range(8):
            row = jnp.broadcast_to(block_taps[g : g + 1, :], (TAPS, TAPS))
            turned = pltpu.roll(row, 0, 1, stride=1, stride_axis=0)
            table = jnp.concatenate(
                [jnp.where(later, turned, 0.0), jnp.where(later, 0.0, turned)], axis=1
            ).astype(BF16)
            conv = jnp.where(
                lane_group == g, jnp.dot(table, window, preferred_element_type=F32), conv
            )
        for b in range(2):
            rows = pl.ds(b * TAPS, TAPS)
            source = mrx[TAPS + b * TAPS : 2 * TAPS + b * TAPS, cols].astype(F32)
            total = conv[:, b * TAPS : (b + 1) * TAPS] + ms[0:1, cols] * source
            mro[rows, cols] = (ld[5, rows, cols].astype(F32) * total).astype(BF16)
        return 0

    def forward(src_chip):
        piece = kv.at[src_chip, :, own_rows]
        return remote(
            piece, piece, fwd_send.at[src_chip], fwd_recv.at[src_chip], ctx=sib
        )

    sib_rows = pl.ds(pl.multiple_of((1 - core) * ROWS, ROWS), ROWS)

    def take(src_chip):
        for part in range(2):
            arrived(
                kv.at[src_chip, part, own_rows], fwd_send.at[src_chip], kv_recv.at[src_chip, part]
            )
        forward(src_chip).start()

    take(chip)

    def query_here(i, _):
        tops[i] = jnp.full((ROWS, HEAD), -1e30, F32)
        norms[i] = jnp.zeros((ROWS, HEAD), F32)
        mixes[i] = jnp.zeros((ROWS, HEAD), F32)
        arrived(qb.at[i], q_send.at[0], q_recv.at[i])
        return 0

    lax.fori_loop(0, 8, query_here, 0)

    q_row = lax.broadcasted_iota(jnp.int32, (ROWS, 2 * ROWS), 0)
    k_row = lax.broadcasted_iota(jnp.int32, (ROWS, 2 * ROWS), 1)

    def attend(chunk, slot, last_key=None):
        s = lax.dot_general(
            qb[slot], kv[chunk, 0], (((1,), (1,)), ((), ())), preferred_element_type=F32
        )
        if last_key is not None:
            s = jnp.where(k_row <= q_row + last_key, s, -1e30)
        old = tops[slot]
        new = jnp.maximum(old, jnp.max(s, axis=1, keepdims=True))
        factor = jnp.exp2((old - new) * EXP_SCALE)
        expo = jnp.exp2((s - jnp.concatenate([new] * 4, axis=1)) * EXP_SCALE)
        tops[slot] = new
        norms[slot] = norms[slot] * factor + (
            expo[:, 0:128] + expo[:, 128:256] + expo[:, 256:384] + expo[:, 384:512]
        )
        mixes[slot] = mixes[slot] * factor + jnp.dot(
            expo.astype(BF16), kv[chunk, 1], preferred_element_type=F32
        )

    def head_copy(slot):
        half = lax.rem(core + slot, 2)
        return remote(
            ob.at[slot], hb.at[:, head_cols(chip)],
            h_send.at[slot], h_recv.at[chip], ctx=2 * slot + half,
        )

    def stage(n, _):
        src_chip = source(n)

        @pl.when(n < 7)
        def _():
            take(source(n + 1))

        arrived(kv.at[src_chip, :, sib_rows], fwd_send.at[src_chip], fwd_recv.at[src_chip])

        @pl.when(n < 7)
        def _():
            attend(src_chip, src_chip, lax.rem(core + src_chip, 2) * ROWS)

            def rest(slot, _):
                attend(src_chip, slot)
                return 0

            lax.fori_loop(src_chip + 1, 8, rest, 0)

        return 0

    lax.fori_loop(0, 8, stage, 0)
    last_chip = source(7)

    def complete(o, _):
        slot = lax.rem(chip + 1 + o, 8)

        @pl.when(slot >= last_chip)
        def _():
            attend(
                last_chip, slot,
                jnp.where(slot > last_chip, 2 * ROWS, lax.rem(core + slot, 2) * ROWS),
            )

        ob[slot] = (
            mixes[slot] / jnp.sum(norms[slot], axis=1, keepdims=True)
        ).astype(BF16)
        stays = jnp.logical_and(slot == chip, even)

        @pl.when(stays)
        def _():
            pltpu.make_async_copy(ob.at[slot], hb.at[:, head_cols(chip)], h_recv.at[chip]).start()

        @pl.when(jnp.logical_not(stays))
        def _():
            head_copy(slot).start()

        return 0

    lax.fori_loop(0, 8, complete, 0)

    for copy in weights:
        copy.wait()

    def heads_here(i, _):
        arrived(hb.at[:, head_cols(i)], h_send.at[0], h_recv.at[i])
        return 0

    lax.fori_loop(0, 8, heads_here, 0)

    def project(block):
        def columns(n, _):
            cols = pl.ds(pl.multiple_of(n * 256, 256), 256)
            pb[block, :, cols] = jnp.dot(
                hb[...], wb[block, :, cols], preferred_element_type=F32
            ).astype(BF16)
            return 0

        lax.fori_loop(0, CHANS // 256, columns, 0)

    def piece(r):
        return pl.ds(r * PIECE, PIECE)

    put_se = pltpu.make_async_copy(seo, se_out, out_sem.at[0])
    put_mr = pltpu.make_async_copy(mro, mr_out, out_sem.at[1])
    ahead = (zp, zm)
    to = (up, down)

    def far_copy(d, r):
        return remote(
            pb.at[2 * zf + d, piece(r)], far.at[d, piece(r)],
            far_send.at[d, r], far_recv.at[d, r], tp=to[d],
        )

    def near_copy(d, h, r):
        return remote(
            pb.at[2 * ahead[d] + h, piece(r)], near.at[d, h, piece(r)],
            near_send.at[d, h, r], near_recv.at[d, h, r], tp=to[d],
        )

    def side_copy(r):
        return remote(
            fin.at[piece(r)], yb.at[piece(r)], y_send.at[r], y_recv.at[r], tp=side
        )

    def finish(r):
        for d in range(2):
            for h in range(2):
                near_copy(d, h, r).wait_recv()

        def total(h):
            return (
                pb[2 * z + h, piece(r), :].astype(F32)
                + near[0, h, piece(r), :].astype(F32)
                + near[1, h, piece(r), :].astype(F32)
            )

        fin[piece(r), :] = total(1 - yh).astype(BF16)
        side_copy(r).start()
        acc_own[piece(r), :] = total(yh)

    across = (zf, zp, zm, z)

    def g_piece(j):
        return pl.ds(F_ROWS + j * PIECE, PIECE)

    def g_half(j, h):
        return pl.ds(F_ROWS + j * PIECE + h * HALF, HALF)

    def gy_copy(i, j):
        return remote(
            pb.at[2 * across[i] + 1 - yh, g_piece(j)], gy.at[i, pl.ds(j * PIECE, PIECE)],
            gy_send.at[i, j], gy_recv.at[i, j], tp=side,
        )

    def gfar_copy(d, j):
        return remote(
            pb.at[2 * zf + yh, g_half(j, d)], gfar.at[d, j],
            gfar_send.at[d, j], gfar_recv.at[d, j], tp=to[d],
        )

    def gnear_copy(d, merged, j):
        return remote(
            pb.at[2 * ahead[d] + yh, g_half(j, d if merged else 1 - d)], gnear.at[d, merged, j],
            gnear_send.at[d, merged, j], gnear_recv.at[d, merged, j], tp=to[d],
        )

    def g_cross(i):
        for j in range(Y_FIRST):
            gy_copy(i, j).start()

    def g_merge(i, j):
        gy_copy(i, j).wait_recv()
        block = 2 * across[i] + yh
        pb[block, g_piece(j), :] = (
            pb[block, g_piece(j), :].astype(F32)
            + gy[i, pl.ds(j * PIECE, PIECE), :].astype(F32)
        ).astype(BF16)

    project(2 * zf)
    project(2 * zf + 1)
    for r in range(2):
        for d in range(2):
            far_copy(d, r).start()
    g_cross(0)
    project(2 * zp + 1)
    project(2 * zm)
    for d in range(2):
        near_copy(d, 1 - d, 0).start()
    project(2 * zp)
    project(2 * zm + 1)
    project(2 * z)
    project(2 * z + 1)
    @pl.when(c > 0)
    def _():
        arrived(sex.at[pl.ds(0, 8)], halo_send.at[1], halo_recv.at[1])

    @pl.when(c == 0)
    def _():
        sex[0:8, :] = jnp.zeros((8, CHANS), F32)

    loads[4].wait()
    loads[5].wait()

    @pl.when(c > 0)
    def _():
        arrived(mrx.at[pl.ds(0, TAPS)], halo_send.at[0], halo_recv.at[0])

    @pl.when(c == 0)
    def _():
        mrx[0:TAPS, :] = jnp.zeros((TAPS, CHANS), BF16)

    for r in range(Z_FIRST):
        for d in range(2):
            far_copy(d, r).wait_recv()
            block = 2 * ahead[d] + d
            pb[block, piece(r), :] = (
                pb[block, piece(r), :].astype(F32) + far[d, piece(r), :].astype(F32)
            ).astype(BF16)
            near_copy(d, d, r).start()
        for d in range(2):
            if r + 1 < Z_FIRST:
                near_copy(d, 1 - d, r + 1).start()
            if r + 2 < Z_FIRST:
                far_copy(d, r + 2).start()
        if r < 3:
            g_cross(r + 1)
        lax.fori_loop(2 * r, 2 * r + 2, short_block, 0)
        lax.fori_loop(2 * r, 2 * r + 2, medium_block, 0)
        if r == 1:
            for j in range(Y_FIRST):
                g_merge(0, j)
                for d in range(2):
                    gfar_copy(d, j).start()
        if r > 0:
            finish(r - 1)
    put_se.start()
    put_mr.start()
    for i in range(2):
        for j in range(Y_FIRST):
            g_merge(i + 1, j)
            gnear_copy(i, 0, j).start()
    for j in range(Y_FIRST):
        for d in range(2):
            gfar_copy(d, j).wait_recv()
            block = 2 * ahead[d] + yh
            pb[block, g_half(j, d), :] = (
                pb[block, g_half(j, d), :].astype(F32) + gfar[d, j].astype(F32)
            ).astype(BF16)
            gnear_copy(d, 1, j).start()
    finish(Z_FIRST - 1)
    summed = ld.at[0]
    for j in range(Y_FIRST):
        g_merge(3, j)
    for r in range(Z_FIRST):
        side_copy(r).wait_recv()
        summed[piece(r), :] = (
            acc_own[piece(r), :] + yb[piece(r), :].astype(F32)
        ).astype(BF16)
    for j in range(Y_FIRST):
        for d in range(2):
            for merged in range(2):
                gnear_copy(d, merged, j).wait_recv()
        for h in range(2):
            summed[g_half(j, h), :] = (
                pb[2 * z + yh, g_half(j, h), :].astype(F32)
                + gnear[0, 1 - h, j].astype(F32)
                + gnear[1, h, j].astype(F32)
            ).astype(BF16)
    put_attn = pltpu.make_async_copy(ld.at[0], attn_out, out_sem.at[2])
    put_attn.start()

    @pl.when(c < 15)
    def _():
        se_halo.wait_send()
        mr_halo.wait_send()

    for i, (dx, dy) in enumerate(OFFSETS[1:]):
        dest = to_chip(dx, dy)
        kv_copy(i, dest, 0).wait_send()
        kv_copy(i, dest, 1).wait_send()
        q_copy(i, dest).wait_send()

    @pl.when(jnp.logical_not(even))
    def _():
        sib_q.wait_send()

    def forwarded(i, _):
        forward(i).wait_send()
        stays = jnp.logical_and(i == chip, even)

        @pl.when(jnp.logical_not(stays))
        def _():
            head_copy(i).wait_send()

        return 0

    lax.fori_loop(0, 8, forwarded, 0)
    for d in range(2):
        for r in range(Z_FIRST):
            far_copy(d, r).wait_send()
            for h in range(2):
                near_copy(d, h, r).wait_send()
        for j in range(Y_FIRST):
            gfar_copy(d, j).wait_send()
            for merged in range(2):
                gnear_copy(d, merged, j).wait_send()
    for r in range(Z_FIRST):
        side_copy(r).wait_send()
    for j in range(Y_FIRST):
        for i in range(4):
            gy_copy(i, j).wait_send()
    put_se.wait()
    put_mr.wait()
    put_attn.wait()


def hand_over(a, b, c, a_out, b_out, c_out, held, in_sem, put_sem):
    pairs = ((a, a_out), (b, b_out), (c, c_out))
    gets = [
        pltpu.make_async_copy(src, held.at[i], in_sem.at[i]) for i, (src, _) in enumerate(pairs)
    ]
    puts = [
        pltpu.make_async_copy(held.at[i], dst, put_sem.at[i]) for i, (_, dst) in enumerate(pairs)
    ]
    for get in gets:
        get.start()
    for get, put in zip(gets, puts):
        get.wait()
        put.start()
    for put in puts:
        put.wait()


def local(*args):
    (sq, sk, sv, sf, ss, mq, mk, mv, mf, md, ms, q, k, v, w) = args
    any_spec = pl.BlockSpec(memory_space=pl.ANY)
    vmem = pl.BlockSpec(memory_space=pltpu.VMEM)
    out = jax.ShapeDtypeStruct((ROWS, CHANS), BF16)
    dma = pltpu.SemaphoreType.DMA
    outs = pl.pallas_call(
        kernel,
        name="mixers",
        out_shape=(out, out, out),
        in_specs=[any_spec] * 3 + [vmem] * 2 + [any_spec] * 3 + [vmem] * 3 + [any_spec] * 4,
        out_specs=(any_spec,) * 3,
        scratch_shapes=[
            pltpu.VMEM((6, ROWS, CHANS), BF16),
            pltpu.VMEM((8 + ROWS, CHANS), F32),
            pltpu.VMEM((8, CHANS), F32),
            pltpu.VMEM((TAPS + ROWS, CHANS), BF16),
            pltpu.VMEM((64, TAPS), F32),
            pltpu.VMEM((ROWS, CHANS), BF16),
            pltpu.VMEM((ROWS, CHANS), BF16),
            pltpu.VMEM((8, 2, 2 * ROWS, HEAD), BF16),
            pltpu.VMEM((8, ROWS, HEAD), BF16),
            pltpu.VMEM((8, ROWS, HEAD), BF16),
            pltpu.VMEM((ROWS, CHANS), BF16),
            pltpu.VMEM((8, CHANS, CHANS), BF16),
            pltpu.VMEM((8, ROWS, CHANS), BF16),
            pltpu.VMEM((8, ROWS, HEAD), F32),
            pltpu.VMEM((8, ROWS, HEAD), F32),
            pltpu.VMEM((8, ROWS, HEAD), F32),
            pltpu.VMEM((2, F_ROWS, CHANS), BF16),
            pltpu.VMEM((2, 2, F_ROWS, CHANS), BF16),
            pltpu.VMEM((F_ROWS, CHANS), BF16),
            pltpu.VMEM((F_ROWS, CHANS), BF16),
            pltpu.VMEM((F_ROWS, CHANS), F32),
            pltpu.VMEM((4, G_ROWS, CHANS), BF16),
            pltpu.VMEM((2, Y_FIRST, HALF, CHANS), BF16),
            pltpu.VMEM((2, 2, Y_FIRST, HALF, CHANS), BF16),
            dma((6,)), dma((3,)), dma((8,)),
            dma((2,)), dma((2,)),
            dma((7, 2)), dma((8, 2)), dma((8,)), dma((8,)),
            dma((8,)), dma((8,)), dma((8,)), dma((8,)),
            dma((2, Z_FIRST)), dma((2, Z_FIRST)),
            dma((2, 2, Z_FIRST)), dma((2, 2, Z_FIRST)),
            dma((Z_FIRST,)), dma((Z_FIRST,)),
            dma((4, Y_FIRST)), dma((4, Y_FIRST)),
            dma((2, Y_FIRST)), dma((2, Y_FIRST)),
            dma((2, 2, Y_FIRST)), dma((2, 2, Y_FIRST)),
        ],
        compiler_params=pltpu.CompilerParams(
            collective_id=0, has_side_effects=True, vmem_limit_bytes=56 * 1024 * 1024
        ),
        cost_estimate=pl.CostEstimate(
            flops=12 * 10**9, bytes_accessed=28 * 2**20, transcendentals=5 * 10**6
        ),
    )(
        sq, sk, sv, sf.T, ss.reshape(1, CHANS), mq, mk, mv, mf, md.reshape(1, 64),
        ms.reshape(1, CHANS), q, k, v, w,
    )
    return pl.pallas_call(
        hand_over,
        name="hand_over",
        out_shape=(out, out, out),
        in_specs=[any_spec] * 3,
        out_specs=(any_spec,) * 3,
        scratch_shapes=[pltpu.VMEM((3, ROWS, CHANS), BF16), dma((3,)), dma((3,))],
        cost_estimate=pl.CostEstimate(flops=0, bytes_accessed=3 * 2**20, transcendentals=0),
    )(*outs)


def solution(mesh):
    block = P("ctx", "tp")
    in_specs = (
        block, block, block, P("tp", None), P("tp"),
        block, block, block, P("tp", None), P("tp"), P("tp"),
        block, block, block, P("tp", None),
    )
    return jax.shard_map(
        local, mesh=mesh, in_specs=in_specs, out_specs=(block, block, block), check_vma=False
    )
```

```python
import functools
import math

import jax
import jax.numpy as jnp
from jax import lax
from jax.experimental import pallas as pl
from jax.experimental.pallas import tpu as pltpu
from jax.sharding import PartitionSpec as P

F32 = jnp.float32
BF16 = jnp.bfloat16
HEAD = 128
ROWS = 256
CHANS = 1024
TAPS = 128
SHORT = 7
PIECE = 128
HALF = PIECE // 2
Z_FIRST = 1
Y_FIRST = ROWS // PIECE - Z_FIRST
F_ROWS = Z_FIRST * PIECE
G_ROWS = Y_FIRST * PIECE
EXP_SCALE = HEAD ** (-0.5) * math.log2(math.e)
FLIPS = (7, 1, 6, 2, 5, 3, 4)


def kernel(
    sq, sk, sv, sf_in, ss_in, mq, mk, mv, mf_in, md_in, ms_in, q, k, v, w,
    se_out, mr_out, attn_out,
    ld, sf, ss, mf, md, ms, sex, fexp, mrx, rtap, kv, qb, ob, hb, wb, pb, tops, norms, mixes, score_a, score_b,
    far, near, fin, yb, acc_own, gy, gfar, gnear,
    ld_sem, small_sem, w_sem,
    halo_send, halo_recv,
    kv_send, kv_recv, fwd_send, fwd_recv, q_send, q_recv, h_send, h_recv,
    far_send, far_recv, near_send, near_recv, y_send, y_recv,
    gy_send, gy_recv, gfar_send, gfar_recv, gnear_send, gnear_recv,
):
    c = lax.axis_index("ctx")
    t = lax.axis_index("tp")
    core = lax.rem(c, 2)
    chip = c // 2
    px = lax.rem(chip, 4)
    py = chip // 4
    sib = c + 1 - 2 * core
    z = t // 2
    yh = lax.rem(t, 2)
    zp = lax.rem(z + 1, 4)
    zm = lax.rem(z + 3, 4)
    zf = lax.rem(z + 2, 4)
    up = 2 * zp + yh
    down = 2 * zm + yh
    side = 2 * z + 1 - yh

    def remote(src, dst, send, recv, **where):
        return pltpu.make_async_remote_copy(
            src_ref=src, dst_ref=dst, send_sem=send, recv_sem=recv,
            device_id=where, device_id_type=pl.DeviceIdType.MESH,
        )

    def arrived(dst, send, recv):
        remote(dst, dst, send, recv, ctx=sib).wait_recv()

    barrier = pltpu.get_barrier_semaphore()

    def greet(i, _):
        pl.semaphore_signal(
            barrier, inc=1, device_id={"ctx": lax.rem(c + i, 16)},
            device_id_type=pl.DeviceIdType.MESH,
        )
        return 0

    lax.fori_loop(1, 16, greet, 0)
    for peer in (up, down, side):
        pl.semaphore_signal(
            barrier, inc=1, device_id={"tp": peer}, device_id_type=pl.DeviceIdType.MESH
        )

    loads = [
        pltpu.make_async_copy(src, ld.at[i], ld_sem.at[i])
        for i, src in enumerate((mk, mv, sk, sv, sq, mq))
    ]
    for copy in loads:
        copy.start()

    pl.semaphore_wait(barrier, 18)

    own_rows = pl.ds(pl.multiple_of(core * ROWS, ROWS), ROWS)
    q_core = lax.rem(core + chip, 2)

    def head_cols(h):
        return pl.ds(pl.multiple_of(h * HEAD, HEAD), HEAD)

    def flipped(flip):
        bits = (lax.rem(px, 2), px // 2, py)
        out = 0
        for i, bit in enumerate(bits):
            m = flip // 2**i % 2
            out = out + 2**i * (bit + m - 2 * bit * m)
        return out

    def kv_copy(i, dest, part):
        return remote(
            (k, v)[part].at[:, head_cols(dest)], kv.at[chip, part, own_rows],
            kv_send.at[i, part], kv_recv.at[chip, part], ctx=2 * dest + core,
        )

    def q_copy(i, dest):
        return remote(
            q.at[:, head_cols(dest)], qb.at[chip],
            q_send.at[i], q_recv.at[chip], ctx=2 * dest + q_core,
        )

    def send_kv(first, last):
        for i in range(first, last):
            kv_copy(i, flipped(FLIPS[i]), 0).start()
            kv_copy(i, flipped(FLIPS[i]), 1).start()

    for i, flip in enumerate(FLIPS):
        q_copy(i, flipped(flip)).start()
    send_kv(0, 1)
    own_kv = [
        pltpu.make_async_copy(
            src.at[:, head_cols(chip)], kv.at[chip, part, own_rows], kv_recv.at[chip, part]
        )
        for part, src in enumerate((k, v))
    ]
    for copy in own_kv:
        copy.start()
    own_q = pltpu.make_async_copy(q.at[:, head_cols(chip)], qb.at[chip], q_recv.at[chip])
    sib_q = remote(
        q.at[:, head_cols(chip)], qb.at[chip], q_send.at[7], q_recv.at[chip], ctx=sib
    )
    even = lax.rem(chip, 2) == 0

    @pl.when(even)
    def _():
        own_q.start()

    @pl.when(jnp.logical_not(even))
    def _():
        sib_q.start()

    small = [
        pltpu.make_async_copy(src, dst, small_sem.at[i])
        for i, (src, dst) in enumerate(
            ((sf_in, sf), (ss_in, ss), (mf_in, mf), (md_in, md), (ms_in, ms))
        )
    ]
    for copy in small:
        copy.start()

    def product(first, second, r):
        rows = pl.ds(pl.multiple_of(r * 32, 32), 32)
        return (ld[first, rows, :].astype(F32) * ld[second, rows, :].astype(F32)).astype(BF16)

    loads[0].wait()
    loads[1].wait()

    def mr_product(r, _):
        mrx[pl.ds(pl.multiple_of(TAPS + r * 32, 32), 32), :] = product(0, 1, r)
        return 0

    lax.fori_loop(0, ROWS // 32, mr_product, 0)
    loads[2].wait()
    loads[3].wait()

    def se_product(r, _):
        sex[pl.ds(pl.multiple_of(8 + r * 32, 8), 32), :] = product(2, 3, r).astype(F32)
        return 0

    lax.fori_loop(0, ROWS // 32, se_product, 0)

    mr_halo = remote(
        mrx.at[pl.ds(ROWS, TAPS)], mrx.at[pl.ds(0, TAPS)],
        halo_send.at[0], halo_recv.at[0], ctx=lax.rem(c + 1, 16),
    )
    se_halo = remote(
        sex.at[pl.ds(ROWS, 8)], sex.at[pl.ds(0, 8)],
        halo_send.at[1], halo_recv.at[1], ctx=lax.rem(c + 1, 16),
    )

    send_kv(1, 3)
    weights = [
        pltpu.make_async_copy(w.at[:, pl.ds(i * CHANS, CHANS)], wb.at[i], w_sem.at[i])
        for i in range(8)
    ]
    for copy in weights:
        copy.start()

    for copy in small:
        copy.wait()

    group_of = lax.broadcasted_iota(jnp.int32, (64, CHANS), 1) // 16
    mine = group_of == lax.broadcasted_iota(jnp.int32, (64, CHANS), 0)
    row64 = lax.broadcasted_iota(jnp.int32, (64, 64), 0)
    lane64 = lax.broadcasted_iota(jnp.int32, (64, 64), 1)

    def as_column(row):
        return jnp.sum(jnp.where(row64 == lane64, row, 0.0), axis=1, keepdims=True)

    for j in range(SHORT):
        fexp[j : j + 1, :] = jnp.sum(
            jnp.where(mine, as_column(sf[j : j + 1, :]), 0.0), axis=0, keepdims=True
        )

    def short_block(l, _):
        cols = pl.ds(pl.multiple_of(l * 128, 128), 128)
        conv = sex[8 : 8 + ROWS, cols] * fexp[0:1, cols]
        for j in range(1, SHORT):
            conv = conv + sex[8 - j : 8 - j + ROWS, cols] * fexp[j : j + 1, cols]
        skipped = ss[0:1, cols] * sex[8 : 8 + ROWS, cols]
        se_out[:, cols] = (ld[4, :, cols].astype(F32) * (conv + skipped)).astype(BF16)
        return 0

    decay = as_column(md[...])
    tap_index = lax.broadcasted_iota(jnp.int32, (64, TAPS), 1).astype(F32)
    taps = (mf[...] * jnp.exp(-decay * tap_index)).astype(BF16)
    r128 = lax.broadcasted_iota(jnp.int32, (TAPS, TAPS), 0)
    l128 = lax.broadcasted_iota(jnp.int32, (TAPS, TAPS), 1)
    flip = jnp.where(lax.rem(r128 + l128, TAPS) == 0, 1.0, 0.0).astype(BF16)
    rtap[...] = jnp.dot(taps, flip, preferred_element_type=F32)

    later = l128 > r128
    lane_group = lax.rem(lax.broadcasted_iota(jnp.int32, (TAPS, 2 * TAPS), 1), TAPS) // 16

    def medium_block(l, _):
        cols = pl.ds(pl.multiple_of(l * 128, 128), 128)
        window = jnp.concatenate(
            [mrx[0 : 2 * TAPS, cols], mrx[TAPS : 3 * TAPS, cols]], axis=1
        )
        block_taps = rtap[pl.ds(pl.multiple_of(l * 8, 8), 8), :]
        conv = jnp.zeros((TAPS, 2 * TAPS), F32)
        for g in range(8):
            row = jnp.broadcast_to(block_taps[g : g + 1, :], (TAPS, TAPS))
            turned = pltpu.roll(row, 0, 1, stride=1, stride_axis=0)
            table = jnp.concatenate(
                [jnp.where(later, turned, 0.0), jnp.where(later, 0.0, turned)], axis=1
            ).astype(BF16)
            conv = jnp.where(
                lane_group == g, jnp.dot(table, window, preferred_element_type=F32), conv
            )
        for b in range(2):
            rows = pl.ds(b * TAPS, TAPS)
            source = mrx[TAPS + b * TAPS : 2 * TAPS + b * TAPS, cols].astype(F32)
            total = conv[:, b * TAPS : (b + 1) * TAPS] + ms[0:1, cols] * source
            mr_out[rows, cols] = (ld[5, rows, cols].astype(F32) * total).astype(BF16)
        return 0

    def forward(src_chip):
        piece = kv.at[src_chip, :, own_rows]
        return remote(
            piece, piece, fwd_send.at[src_chip], fwd_recv.at[src_chip], ctx=sib
        )

    sib_rows = pl.ds(pl.multiple_of((1 - core) * ROWS, ROWS), ROWS)

    def take(src_chip):
        for part in range(2):
            arrived(
                kv.at[src_chip, part, own_rows], fwd_send.at[src_chip], kv_recv.at[src_chip, part]
            )
        forward(src_chip).start()

    def query_here(i, _):
        tops[i] = jnp.full((ROWS, HEAD), -1e30, F32)
        norms[i] = jnp.zeros((ROWS, HEAD), F32)
        mixes[i] = jnp.zeros((ROWS, HEAD), F32)
        arrived(qb.at[i], q_send.at[0], q_recv.at[i])
        return 0

    lax.fori_loop(0, 8, query_here, 0)
    send_kv(3, 5)

    q_row = lax.broadcasted_iota(jnp.int32, (ROWS, 2 * ROWS), 0)
    k_row = lax.broadcasted_iota(jnp.int32, (ROWS, 2 * ROWS), 1)

    def weigh(scores, chunk, slot, masked):
        s = scores[...]
        if masked:
            limit = jnp.where(slot == chunk, lax.rem(core + slot, 2) * ROWS, 2 * ROWS)
            s = jnp.where(k_row <= q_row + limit, s, -1e30)
        old = tops[slot]
        new = jnp.maximum(old, jnp.max(s, axis=1, keepdims=True))
        factor = jnp.exp2((old - new) * EXP_SCALE)
        expo = jnp.exp2((s - jnp.concatenate([new] * 4, axis=1)) * EXP_SCALE)
        mixed = jnp.dot(expo.astype(BF16), kv[chunk, 1], preferred_element_type=F32)
        tops[slot] = new
        norms[slot] = norms[slot] * factor + (
            expo[:, 0:128] + expo[:, 128:256] + expo[:, 256:384] + expo[:, 384:512]
        )
        mixes[slot] = mixes[slot] * factor + mixed

    def wave(m, _):
        first = flipped(m)
        low = jnp.minimum(first, 7 - first)
        high = 7 - low
        take(first)
        take(7 - first)

        @pl.when(m == 0)
        def _():
            send_kv(5, 7)

        for src_chip in (first, 7 - first):
            arrived(kv.at[src_chip, :, sib_rows], fwd_send.at[src_chip], fwd_recv.at[src_chip])

        def step(j):
            of_low = j < 8 - low
            return jnp.where(of_low, low, high), jnp.where(of_low, low + j, j - 1)

        def score(j):
            chunk, slot = step(j)
            (score_a, score_b)[j % 2][...] = lax.dot_general(
                qb[slot], kv[chunk, 0], (((1,), (1,)), ((), ())), preferred_element_type=F32
            )

        score(0)
        for j in range(9):
            if j < 8:
                score(j + 1)
            weigh((score_a, score_b)[j % 2], *step(j), j == 0 or j > 4)
        return 0

    lax.fori_loop(0, 4, wave, 0)

    def rows_of(half):
        return pl.ds(half * F_ROWS, F_ROWS if half == 0 else G_ROWS)

    def head_copy(slot, half):
        return remote(
            ob.at[slot, rows_of(half)], hb.at[rows_of(half), head_cols(chip)],
            h_send.at[slot, half], h_recv.at[chip, half],
            ctx=2 * slot + lax.rem(core + slot, 2),
        )

    def give_back(slot, half):
        stays = jnp.logical_and(slot == chip, even)

        @pl.when(stays)
        def _():
            pltpu.make_async_copy(
                ob.at[slot, rows_of(half)], hb.at[rows_of(half), head_cols(chip)],
                h_recv.at[chip, half],
            ).start()

        @pl.when(jnp.logical_not(stays))
        def _():
            head_copy(slot, half).start()

    def complete(half):
        def one(o, _):
            slot = lax.rem(chip + 1 + o, 8)
            rows = rows_of(half)
            ob[slot, rows, :] = (
                mixes[slot, rows, :] / jnp.sum(norms[slot, rows, :], axis=1, keepdims=True)
            ).astype(BF16)
            if half == 1:
                give_back(slot, half)
            return 0

        lax.fori_loop(0, 8, one, 0)

    def heads_here(half):
        def one(i, _):
            arrived(hb.at[rows_of(half), head_cols(i)], h_send.at[0, half], h_recv.at[i, half])
            return 0

        lax.fori_loop(0, 8, one, 0)

    complete(1)
    complete(0)

    def second_half(o, _):
        slot = lax.rem(chip + 1 + o, 8)

        @pl.when(jnp.logical_not(jnp.logical_and(slot == chip, even)))
        def _():
            head_copy(slot, 1).wait_send()

        give_back(slot, 0)
        return 0

    lax.fori_loop(0, 8, second_half, 0)

    @pl.when(c < 15)
    def _():
        se_halo.start()
        mr_halo.start()

    for copy in weights:
        copy.wait()
    heads_here(1)

    every = pl.ds(0, ROWS)

    def project(block, rows):
        def columns(n, _):
            cols = pl.ds(pl.multiple_of(n * 256, 256), 256)
            pb[block, rows, cols] = jnp.dot(
                hb[rows, :], wb[block, :, cols], preferred_element_type=F32
            ).astype(BF16)
            return 0

        lax.fori_loop(0, CHANS // 256, columns, 0)

    def piece(r):
        return pl.ds(r * PIECE, PIECE)

    ahead = (zp, zm)
    to = (up, down)

    def far_copy(d, r):
        return remote(
            pb.at[2 * zf + d, piece(r)], far.at[d, piece(r)],
            far_send.at[d, r], far_recv.at[d, r], tp=to[d],
        )

    def near_copy(d, h, r):
        return remote(
            pb.at[2 * ahead[d] + h, piece(r)], near.at[d, h, piece(r)],
            near_send.at[d, h, r], near_recv.at[d, h, r], tp=to[d],
        )

    def side_copy(r):
        return remote(
            fin.at[piece(r)], yb.at[piece(r)], y_send.at[r], y_recv.at[r], tp=side
        )

    def finish(r):
        for d in range(2):
            for h in range(2):
                near_copy(d, h, r).wait_recv()

        def total(h):
            return (
                pb[2 * z + h, piece(r), :].astype(F32)
                + near[0, h, piece(r), :].astype(F32)
                + near[1, h, piece(r), :].astype(F32)
            )

        fin[piece(r), :] = total(1 - yh).astype(BF16)
        side_copy(r).start()
        acc_own[piece(r), :] = total(yh)

    across = (zf, zp, zm, z)

    def g_piece(j):
        return pl.ds(F_ROWS + j * PIECE, PIECE)

    def g_half(j, h):
        return pl.ds(F_ROWS + j * PIECE + h * HALF, HALF)

    def gy_copy(i, j):
        return remote(
            pb.at[2 * across[i] + 1 - yh, g_piece(j)], gy.at[i, pl.ds(j * PIECE, PIECE)],
            gy_send.at[i, j], gy_recv.at[i, j], tp=side,
        )

    def gfar_copy(d, j):
        return remote(
            pb.at[2 * zf + yh, g_half(j, d)], gfar.at[d, j],
            gfar_send.at[d, j], gfar_recv.at[d, j], tp=to[d],
        )

    def gnear_copy(d, merged, j):
        return remote(
            pb.at[2 * ahead[d] + yh, g_half(j, d if merged else 1 - d)], gnear.at[d, merged, j],
            gnear_send.at[d, merged, j], gnear_recv.at[d, merged, j], tp=to[d],
        )

    def g_cross(i):
        for j in range(Y_FIRST):
            gy_copy(i, j).start()

    def g_merge(i, j):
        gy_copy(i, j).wait_recv()
        block = 2 * across[i] + yh
        pb[block, g_piece(j), :] = (
            pb[block, g_piece(j), :].astype(F32)
            + gy[i, pl.ds(j * PIECE, PIECE), :].astype(F32)
        ).astype(BF16)

    project(2 * zf + 1 - yh, rows_of(1))
    g_cross(0)
    heads_here(0)
    for h in range(2):
        project(2 * zf + h, rows_of(0))
    for r in range(1):
        for d in range(2):
            far_copy(d, r).start()
    project(2 * zp + 1, rows_of(0))
    project(2 * zm, rows_of(0))
    for d in range(2):
        near_copy(d, 1 - d, 0).start()
    project(2 * zp + 1 - yh, rows_of(1))
    g_cross(1)
    project(2 * zp, rows_of(0))
    project(2 * zm + 1, rows_of(0))
    for i in range(1, 3):
        project(2 * across[i] + yh, rows_of(1))
    project(2 * zm + 1 - yh, rows_of(1))
    project(2 * zf + yh, rows_of(1))
    project(2 * z, every)
    project(2 * z + 1, every)

    @pl.when(c > 0)
    def _():
        arrived(sex.at[pl.ds(0, 8)], halo_send.at[1], halo_recv.at[1])

    @pl.when(c == 0)
    def _():
        sex[0:8, :] = jnp.zeros((8, CHANS), F32)

    loads[4].wait()
    loads[5].wait()

    for r in range(Z_FIRST):
        for d in range(2):
            far_copy(d, r).wait_recv()
            block = 2 * ahead[d] + d
            pb[block, piece(r), :] = (
                pb[block, piece(r), :].astype(F32) + far[d, piece(r), :].astype(F32)
            ).astype(BF16)
            near_copy(d, d, r).start()
        for d in range(2):
            if r + 1 < Z_FIRST:
                near_copy(d, 1 - d, r + 1).start()
            if r + 2 < Z_FIRST:
                far_copy(d, r + 2).start()
        g_cross(2)
        g_cross(3)
        if r == 0:
            lax.fori_loop(0, 8, short_block, 0)
        for j in range(Y_FIRST):
            g_merge(0, j)
            for d in range(2):
                gfar_copy(d, j).start()
        @pl.when(c > 0)
        def _():
            arrived(mrx.at[pl.ds(0, TAPS)], halo_send.at[0], halo_recv.at[0])

        @pl.when(c == 0)
        def _():
            mrx[0:TAPS, :] = jnp.zeros((TAPS, CHANS), BF16)
        lax.fori_loop(0, 8, medium_block, 0)
    for i in range(2):
        for j in range(Y_FIRST):
            g_merge(i + 1, j)
            gnear_copy(i, 0, j).start()
    for j in range(Y_FIRST):
        for d in range(2):
            gfar_copy(d, j).wait_recv()
            block = 2 * ahead[d] + yh
            pb[block, g_half(j, d), :] = (
                pb[block, g_half(j, d), :].astype(F32) + gfar[d, j].astype(F32)
            ).astype(BF16)
            gnear_copy(d, 1, j).start()
    finish(Z_FIRST - 1)
    for j in range(Y_FIRST):
        g_merge(3, j)
    for r in range(Z_FIRST):
        side_copy(r).wait_recv()
        attn_out[piece(r), :] = (
            acc_own[piece(r), :] + yb[piece(r), :].astype(F32)
        ).astype(BF16)
    for j in range(Y_FIRST):
        for d in range(2):
            for merged in range(2):
                gnear_copy(d, merged, j).wait_recv()
        for h in range(2):
            attn_out[g_half(j, h), :] = (
                pb[2 * z + yh, g_half(j, h), :].astype(F32)
                + gnear[0, 1 - h, j].astype(F32)
                + gnear[1, h, j].astype(F32)
            ).astype(BF16)

    @pl.when(c < 15)
    def _():
        se_halo.wait_send()
        mr_halo.wait_send()

    for i, flip in enumerate(FLIPS):
        dest = flipped(flip)
        kv_copy(i, dest, 0).wait_send()
        kv_copy(i, dest, 1).wait_send()
        q_copy(i, dest).wait_send()

    @pl.when(jnp.logical_not(even))
    def _():
        sib_q.wait_send()

    def forwarded(i, _):
        forward(i).wait_send()
        stays = jnp.logical_and(i == chip, even)

        @pl.when(jnp.logical_not(stays))
        def _():
            head_copy(i, 0).wait_send()

        return 0

    lax.fori_loop(0, 8, forwarded, 0)
    for d in range(2):
        for r in range(Z_FIRST):
            far_copy(d, r).wait_send()
            for h in range(2):
                near_copy(d, h, r).wait_send()
        for j in range(Y_FIRST):
            gfar_copy(d, j).wait_send()
            for merged in range(2):
                gnear_copy(d, merged, j).wait_send()
    for r in range(Z_FIRST):
        side_copy(r).wait_send()
    for j in range(Y_FIRST):
        for i in range(4):
            gy_copy(i, j).wait_send()


def local(*args):
    (sq, sk, sv, sf, ss, mq, mk, mv, mf, md, ms, q, k, v, w) = args
    any_spec = pl.BlockSpec(memory_space=pl.ANY)
    vmem = pl.BlockSpec(memory_space=pltpu.VMEM)
    out = jax.ShapeDtypeStruct((ROWS, CHANS), BF16)
    dma = pltpu.SemaphoreType.DMA
    outs = pl.pallas_call(
        kernel,
        name="mixers",
        out_shape=(pltpu.VMEM((ROWS, CHANS), BF16),) * 3,
        in_specs=[any_spec] * 15,
        out_specs=(vmem,) * 3,
        scratch_shapes=[
            pltpu.VMEM((6, ROWS, CHANS), BF16),
            pltpu.VMEM((SHORT, 64), F32),
            pltpu.VMEM((1, CHANS), F32),
            pltpu.VMEM((64, TAPS), F32),
            pltpu.VMEM((1, 64), F32),
            pltpu.VMEM((1, CHANS), F32),
            pltpu.VMEM((8 + ROWS, CHANS), F32),
            pltpu.VMEM((8, CHANS), F32),
            pltpu.VMEM((TAPS + ROWS, CHANS), BF16),
            pltpu.VMEM((64, TAPS), F32),
            pltpu.VMEM((8, 2, 2 * ROWS, HEAD), BF16),
            pltpu.VMEM((8, ROWS, HEAD), BF16),
            pltpu.VMEM((8, ROWS, HEAD), BF16),
            pltpu.VMEM((ROWS, CHANS), BF16),
            pltpu.VMEM((8, CHANS, CHANS), BF16),
            pltpu.VMEM((8, ROWS, CHANS), BF16),
            pltpu.VMEM((8, ROWS, HEAD), F32),
            pltpu.VMEM((8, ROWS, HEAD), F32),
            pltpu.VMEM((8, ROWS, HEAD), F32),
            pltpu.VMEM((ROWS, 2 * ROWS), F32),
            pltpu.VMEM((ROWS, 2 * ROWS), F32),
            pltpu.VMEM((2, F_ROWS, CHANS), BF16),
            pltpu.VMEM((2, 2, F_ROWS, CHANS), BF16),
            pltpu.VMEM((F_ROWS, CHANS), BF16),
            pltpu.VMEM((F_ROWS, CHANS), BF16),
            pltpu.VMEM((F_ROWS, CHANS), F32),
            pltpu.VMEM((4, G_ROWS, CHANS), BF16),
            pltpu.VMEM((2, Y_FIRST, HALF, CHANS), BF16),
            pltpu.VMEM((2, 2, Y_FIRST, HALF, CHANS), BF16),
            dma((6,)), dma((5,)), dma((8,)),
            dma((2,)), dma((2,)),
            dma((7, 2)), dma((8, 2)), dma((8,)), dma((8,)),
            dma((8,)), dma((8,)), dma((8, 2)), dma((8, 2)),
            dma((2, Z_FIRST)), dma((2, Z_FIRST)),
            dma((2, 2, Z_FIRST)), dma((2, 2, Z_FIRST)),
            dma((Z_FIRST,)), dma((Z_FIRST,)),
            dma((4, Y_FIRST)), dma((4, Y_FIRST)),
            dma((2, Y_FIRST)), dma((2, Y_FIRST)),
            dma((2, 2, Y_FIRST)), dma((2, 2, Y_FIRST)),
        ],
        compiler_params=pltpu.CompilerParams(
            collective_id=0, has_side_effects=True, vmem_limit_bytes=56 * 1024 * 1024
        ),
        cost_estimate=pl.CostEstimate(
            flops=12 * 10**9, bytes_accessed=28 * 2**20, transcendentals=5 * 10**6
        ),
    )(
        sq, sk, sv, sf.T, ss.reshape(1, CHANS), mq, mk, mv, mf, md.reshape(1, 64),
        ms.reshape(1, CHANS), q, k, v, w,
    )
    return outs


def solution(mesh):
    block = P("ctx", "tp")
    in_specs = (
        block, block, block, P("tp", None), P("tp"),
        block, block, block, P("tp", None), P("tp"), P("tp"),
        block, block, block, P("tp", None),
    )
    return jax.shard_map(
        local, mesh=mesh, in_specs=in_specs, out_specs=(block, block, block), check_vma=False
    )
```

```python
import functools
import math

import jax
import jax.numpy as jnp
from jax import lax
from jax.experimental import pallas as pl
from jax.experimental.pallas import tpu as pltpu
from jax.sharding import PartitionSpec as P

F32 = jnp.float32
BF16 = jnp.bfloat16
HEAD = 128
ROWS = 256
CHANS = 1024
TAPS = 128
SHORT = 7
PIECE = 128
HALF = PIECE // 2
Z_FIRST = 1
Y_FIRST = ROWS // PIECE - Z_FIRST
F_ROWS = Z_FIRST * PIECE
G_ROWS = Y_FIRST * PIECE
EXP_SCALE = HEAD ** (-0.5) * math.log2(math.e)
FLIPS = (7, 1, 6, 2, 5, 3, 4)


def kernel(
    sq, sk, sv, sf_in, ss_in, mq, mk, mv, mf_in, md_in, ms_in, q, k, v, w,
    se_out, mr_out, attn_out,
    ld, sf, ss, mf, md, ms, sex, fexp, mrx, rtap, kv, qb, ob, hb, wb, pb, tops, norms, mixes, score_a, score_b,
    far, near, fin, yb, acc_own, gy, gfar, gnear,
    ld_sem, small_sem, w_sem,
    halo_send, halo_recv,
    kv_send, kv_recv, fwd_send, fwd_recv, q_send, q_recv, h_send, h_recv,
    far_send, far_recv, near_send, near_recv, y_send, y_recv,
    gy_send, gy_recv, gfar_send, gfar_recv, gnear_send, gnear_recv,
):
    c = lax.axis_index("ctx")
    t = lax.axis_index("tp")
    core = lax.rem(c, 2)
    chip = c // 2
    px = lax.rem(chip, 4)
    py = chip // 4
    sib = c + 1 - 2 * core
    z = t // 2
    yh = lax.rem(t, 2)
    zp = lax.rem(z + 1, 4)
    zm = lax.rem(z + 3, 4)
    zf = lax.rem(z + 2, 4)
    up = 2 * zp + yh
    down = 2 * zm + yh
    side = 2 * z + 1 - yh

    def remote(src, dst, send, recv, **where):
        return pltpu.make_async_remote_copy(
            src_ref=src, dst_ref=dst, send_sem=send, recv_sem=recv,
            device_id=where, device_id_type=pl.DeviceIdType.MESH,
        )

    def arrived(dst, send, recv):
        remote(dst, dst, send, recv, ctx=sib).wait_recv()

    barrier = pltpu.get_barrier_semaphore()

    def greet(i, _):
        pl.semaphore_signal(
            barrier, inc=1, device_id={"ctx": lax.rem(c + i, 16)},
            device_id_type=pl.DeviceIdType.MESH,
        )
        return 0

    lax.fori_loop(1, 16, greet, 0)
    for peer in (up, down, side):
        pl.semaphore_signal(
            barrier, inc=1, device_id={"tp": peer}, device_id_type=pl.DeviceIdType.MESH
        )

    loads = [
        pltpu.make_async_copy(src, ld.at[i], ld_sem.at[i])
        for i, src in enumerate((mk, mv, sk, sv, sq, mq))
    ]
    for copy in loads:
        copy.start()

    pl.semaphore_wait(barrier, 18)

    own_rows = pl.ds(pl.multiple_of(core * ROWS, ROWS), ROWS)
    q_core = lax.rem(core + chip, 2)

    def head_cols(h):
        return pl.ds(pl.multiple_of(h * HEAD, HEAD), HEAD)

    def flipped(flip):
        bits = (lax.rem(px, 2), px // 2, py)
        out = 0
        for i, bit in enumerate(bits):
            m = flip // 2**i % 2
            out = out + 2**i * (bit + m - 2 * bit * m)
        return out

    def kv_copy(i, dest, part):
        return remote(
            (k, v)[part].at[:, head_cols(dest)], kv.at[chip, part, own_rows],
            kv_send.at[i, part], kv_recv.at[chip, part], ctx=2 * dest + core,
        )

    def q_copy(i, dest):
        return remote(
            q.at[:, head_cols(dest)], qb.at[chip],
            q_send.at[i], q_recv.at[chip], ctx=2 * dest + q_core,
        )

    def send_kv(first, last):
        for i in range(first, last):
            kv_copy(i, flipped(FLIPS[i]), 0).start()
            kv_copy(i, flipped(FLIPS[i]), 1).start()

    for i, flip in enumerate(FLIPS):
        q_copy(i, flipped(flip)).start()
    send_kv(0, 3)
    own_kv = [
        pltpu.make_async_copy(
            src.at[:, head_cols(chip)], kv.at[chip, part, own_rows], kv_recv.at[chip, part]
        )
        for part, src in enumerate((k, v))
    ]
    for copy in own_kv:
        copy.start()
    own_q = pltpu.make_async_copy(q.at[:, head_cols(chip)], qb.at[chip], q_recv.at[chip])
    sib_q = remote(
        q.at[:, head_cols(chip)], qb.at[chip], q_send.at[7], q_recv.at[chip], ctx=sib
    )
    even = lax.rem(chip, 2) == 0

    @pl.when(even)
    def _():
        own_q.start()

    @pl.when(jnp.logical_not(even))
    def _():
        sib_q.start()

    small = [
        pltpu.make_async_copy(src, dst, small_sem.at[i])
        for i, (src, dst) in enumerate(
            ((sf_in, sf), (ss_in, ss), (mf_in, mf), (md_in, md), (ms_in, ms))
        )
    ]
    for copy in small:
        copy.start()

    def product(first, second, r):
        rows = pl.ds(pl.multiple_of(r * 32, 32), 32)
        return (ld[first, rows, :].astype(F32) * ld[second, rows, :].astype(F32)).astype(BF16)

    loads[0].wait()
    loads[1].wait()

    def mr_product(r, _):
        mrx[pl.ds(pl.multiple_of(TAPS + r * 32, 32), 32), :] = product(0, 1, r)
        return 0

    lax.fori_loop(0, ROWS // 32, mr_product, 0)
    loads[2].wait()
    loads[3].wait()

    def se_product(r, _):
        sex[pl.ds(pl.multiple_of(8 + r * 32, 8), 32), :] = product(2, 3, r).astype(F32)
        return 0

    lax.fori_loop(0, ROWS // 32, se_product, 0)

    mr_halo = remote(
        mrx.at[pl.ds(ROWS, TAPS)], mrx.at[pl.ds(0, TAPS)],
        halo_send.at[0], halo_recv.at[0], ctx=lax.rem(c + 1, 16),
    )
    se_halo = remote(
        sex.at[pl.ds(ROWS, 8)], sex.at[pl.ds(0, 8)],
        halo_send.at[1], halo_recv.at[1], ctx=lax.rem(c + 1, 16),
    )

    weights = [
        pltpu.make_async_copy(w.at[:, pl.ds(i * CHANS, CHANS)], wb.at[i], w_sem.at[i])
        for i in range(8)
    ]
    for copy in weights:
        copy.start()

    for copy in small:
        copy.wait()

    group_of = lax.broadcasted_iota(jnp.int32, (64, CHANS), 1) // 16
    mine = group_of == lax.broadcasted_iota(jnp.int32, (64, CHANS), 0)
    row64 = lax.broadcasted_iota(jnp.int32, (64, 64), 0)
    lane64 = lax.broadcasted_iota(jnp.int32, (64, 64), 1)

    def as_column(row):
        return jnp.sum(jnp.where(row64 == lane64, row, 0.0), axis=1, keepdims=True)

    for j in range(SHORT):
        fexp[j : j + 1, :] = jnp.sum(
            jnp.where(mine, as_column(sf[j : j + 1, :]), 0.0), axis=0, keepdims=True
        )

    def short_block(l, _):
        cols = pl.ds(pl.multiple_of(l * 128, 128), 128)
        conv = sex[8 : 8 + ROWS, cols] * fexp[0:1, cols]
        for j in range(1, SHORT):
            conv = conv + sex[8 - j : 8 - j + ROWS, cols] * fexp[j : j + 1, cols]
        skipped = ss[0:1, cols] * sex[8 : 8 + ROWS, cols]
        se_out[:, cols] = (ld[4, :, cols].astype(F32) * (conv + skipped)).astype(BF16)
        return 0

    decay = as_column(md[...])
    tap_index = lax.broadcasted_iota(jnp.int32, (64, TAPS), 1).astype(F32)
    taps = (mf[...] * jnp.exp(-decay * tap_index)).astype(BF16)
    r128 = lax.broadcasted_iota(jnp.int32, (TAPS, TAPS), 0)
    l128 = lax.broadcasted_iota(jnp.int32, (TAPS, TAPS), 1)
    flip = jnp.where(lax.rem(r128 + l128, TAPS) == 0, 1.0, 0.0).astype(BF16)
    rtap[...] = jnp.dot(taps, flip, preferred_element_type=F32)

    later = l128 > r128
    lane_group = lax.rem(lax.broadcasted_iota(jnp.int32, (TAPS, 2 * TAPS), 1), TAPS) // 16

    def medium_block(l, _):
        cols = pl.ds(pl.multiple_of(l * 128, 128), 128)
        window = jnp.concatenate(
            [mrx[0 : 2 * TAPS, cols], mrx[TAPS : 3 * TAPS, cols]], axis=1
        )
        block_taps = rtap[pl.ds(pl.multiple_of(l * 8, 8), 8), :]
        conv = jnp.zeros((TAPS, 2 * TAPS), F32)
        for g in range(8):
            row = jnp.broadcast_to(block_taps[g : g + 1, :], (TAPS, TAPS))
            turned = pltpu.roll(row, 0, 1, stride=1, stride_axis=0)
            table = jnp.concatenate(
                [jnp.where(later, turned, 0.0), jnp.where(later, 0.0, turned)], axis=1
            ).astype(BF16)
            conv = jnp.where(
                lane_group == g, jnp.dot(table, window, preferred_element_type=F32), conv
            )
        for b in range(2):
            rows = pl.ds(b * TAPS, TAPS)
            source = mrx[TAPS + b * TAPS : 2 * TAPS + b * TAPS, cols].astype(F32)
            total = conv[:, b * TAPS : (b + 1) * TAPS] + ms[0:1, cols] * source
            mr_out[rows, cols] = (ld[5, rows, cols].astype(F32) * total).astype(BF16)
        return 0

    def forward(src_chip):
        piece = kv.at[src_chip, :, own_rows]
        return remote(
            piece, piece, fwd_send.at[src_chip], fwd_recv.at[src_chip], ctx=sib
        )

    sib_rows = pl.ds(pl.multiple_of((1 - core) * ROWS, ROWS), ROWS)

    def take(src_chip):
        for part in range(2):
            arrived(
                kv.at[src_chip, part, own_rows], fwd_send.at[src_chip], kv_recv.at[src_chip, part]
            )
        forward(src_chip).start()

    def query_here(i, _):
        tops[i] = jnp.full((ROWS, HEAD), -1e30, F32)
        norms[i] = jnp.zeros((ROWS, HEAD), F32)
        mixes[i] = jnp.zeros((ROWS, HEAD), F32)
        arrived(qb.at[i], q_send.at[0], q_recv.at[i])
        return 0

    lax.fori_loop(0, 8, query_here, 0)
    send_kv(3, 5)

    q_row = lax.broadcasted_iota(jnp.int32, (ROWS, 2 * ROWS), 0)
    k_row = lax.broadcasted_iota(jnp.int32, (ROWS, 2 * ROWS), 1)

    def weigh(scores, chunk, slot, masked):
        s = scores[...]
        if masked:
            limit = jnp.where(slot == chunk, lax.rem(core + slot, 2) * ROWS, 2 * ROWS)
            s = jnp.where(k_row <= q_row + limit, s, -1e30)
        old = tops[slot]
        new = jnp.maximum(old, jnp.max(s, axis=1, keepdims=True))
        factor = jnp.exp2((old - new) * EXP_SCALE)
        expo = jnp.exp2((s - jnp.concatenate([new] * 4, axis=1)) * EXP_SCALE)
        mixed = jnp.dot(expo.astype(BF16), kv[chunk, 1], preferred_element_type=F32)
        tops[slot] = new
        norms[slot] = norms[slot] * factor + (
            expo[:, 0:128] + expo[:, 128:256] + expo[:, 256:384] + expo[:, 384:512]
        )
        mixes[slot] = mixes[slot] * factor + mixed

    def wave(m, _):
        first = flipped(m)
        low = jnp.minimum(first, 7 - first)
        high = 7 - low
        take(first)
        take(7 - first)

        @pl.when(m == 0)
        def _():
            send_kv(5, 7)

        for src_chip in (first, 7 - first):
            arrived(kv.at[src_chip, :, sib_rows], fwd_send.at[src_chip], fwd_recv.at[src_chip])

        def step(j):
            of_low = j < 8 - low
            return jnp.where(of_low, low, high), jnp.where(of_low, low + j, j - 1)

        def score(j):
            chunk, slot = step(j)
            (score_a, score_b)[j % 2][...] = lax.dot_general(
                qb[slot], kv[chunk, 0], (((1,), (1,)), ((), ())), preferred_element_type=F32
            )

        score(0)
        for j in range(9):
            if j < 8:
                score(j + 1)
            weigh((score_a, score_b)[j % 2], *step(j), j == 0 or j > 4)
        return 0

    lax.fori_loop(0, 4, wave, 0)

    def rows_of(half):
        return pl.ds(half * F_ROWS, F_ROWS if half == 0 else G_ROWS)

    def head_copy(slot, half):
        return remote(
            ob.at[slot, rows_of(half)], hb.at[rows_of(half), head_cols(chip)],
            h_send.at[slot, half], h_recv.at[chip, half],
            ctx=2 * slot + lax.rem(core + slot, 2),
        )

    def give_back(slot, half):
        stays = jnp.logical_and(slot == chip, even)

        @pl.when(stays)
        def _():
            pltpu.make_async_copy(
                ob.at[slot, rows_of(half)], hb.at[rows_of(half), head_cols(chip)],
                h_recv.at[chip, half],
            ).start()

        @pl.when(jnp.logical_not(stays))
        def _():
            head_copy(slot, half).start()

    def complete(half):
        def one(o, _):
            slot = lax.rem(chip + 1 + o, 8)
            rows = rows_of(half)
            ob[slot, rows, :] = (
                mixes[slot, rows, :] / jnp.sum(norms[slot, rows, :], axis=1, keepdims=True)
            ).astype(BF16)
            if half == 0:
                give_back(slot, half)
            return 0

        lax.fori_loop(0, 8, one, 0)

    def heads_here(half):
        def one(i, _):
            arrived(hb.at[rows_of(half), head_cols(i)], h_send.at[0, half], h_recv.at[i, half])
            return 0

        lax.fori_loop(0, 8, one, 0)

    complete(0)
    complete(1)

    def second_half(o, _):
        slot = lax.rem(chip + 1 + o, 8)

        @pl.when(jnp.logical_not(jnp.logical_and(slot == chip, even)))
        def _():
            head_copy(slot, 0).wait_send()

        give_back(slot, 1)
        return 0

    lax.fori_loop(0, 8, second_half, 0)

    @pl.when(c < 15)
    def _():
        se_halo.start()
        mr_halo.start()

    for copy in weights:
        copy.wait()
    heads_here(0)

    every = pl.ds(0, ROWS)

    def project(block, rows):
        def columns(n, _):
            cols = pl.ds(pl.multiple_of(n * 256, 256), 256)
            pb[block, rows, cols] = jnp.dot(
                hb[rows, :], wb[block, :, cols], preferred_element_type=F32
            ).astype(BF16)
            return 0

        lax.fori_loop(0, CHANS // 256, columns, 0)

    def piece(r):
        return pl.ds(r * PIECE, PIECE)

    ahead = (zp, zm)
    to = (up, down)

    def far_copy(d, r):
        return remote(
            pb.at[2 * zf + d, piece(r)], far.at[d, piece(r)],
            far_send.at[d, r], far_recv.at[d, r], tp=to[d],
        )

    def near_copy(d, h, r):
        return remote(
            pb.at[2 * ahead[d] + h, piece(r)], near.at[d, h, piece(r)],
            near_send.at[d, h, r], near_recv.at[d, h, r], tp=to[d],
        )

    def side_copy(r):
        return remote(
            fin.at[piece(r)], yb.at[piece(r)], y_send.at[r], y_recv.at[r], tp=side
        )

    def finish(r):
        for d in range(2):
            for h in range(2):
                near_copy(d, h, r).wait_recv()

        def total(h):
            return (
                pb[2 * z + h, piece(r), :].astype(F32)
                + near[0, h, piece(r), :].astype(F32)
                + near[1, h, piece(r), :].astype(F32)
            )

        fin[piece(r), :] = total(1 - yh).astype(BF16)
        side_copy(r).start()
        acc_own[piece(r), :] = total(yh)

    across = (zf, zp, zm, z)

    def g_piece(j):
        return pl.ds(F_ROWS + j * PIECE, PIECE)

    def g_half(j, h):
        return pl.ds(F_ROWS + j * PIECE + h * HALF, HALF)

    def gy_copy(i, j):
        return remote(
            pb.at[2 * across[i] + 1 - yh, g_piece(j)], gy.at[i, pl.ds(j * PIECE, PIECE)],
            gy_send.at[i, j], gy_recv.at[i, j], tp=side,
        )

    def gfar_copy(d, j):
        return remote(
            pb.at[2 * zf + yh, g_half(j, d)], gfar.at[d, j],
            gfar_send.at[d, j], gfar_recv.at[d, j], tp=to[d],
        )

    def gnear_copy(d, merged, j):
        return remote(
            pb.at[2 * ahead[d] + yh, g_half(j, d if merged else 1 - d)], gnear.at[d, merged, j],
            gnear_send.at[d, merged, j], gnear_recv.at[d, merged, j], tp=to[d],
        )

    def g_cross(i):
        for j in range(Y_FIRST):
            gy_copy(i, j).start()

    def g_merge(i, j):
        gy_copy(i, j).wait_recv()
        block = 2 * across[i] + yh
        pb[block, g_piece(j), :] = (
            pb[block, g_piece(j), :].astype(F32)
            + gy[i, pl.ds(j * PIECE, PIECE), :].astype(F32)
        ).astype(BF16)

    for h in range(2):
        project(2 * zf + h, rows_of(0))
    for r in range(1):
        for d in range(2):
            far_copy(d, r).start()
    heads_here(1)
    project(2 * zf + 1 - yh, rows_of(1))
    g_cross(0)
    project(2 * zp + 1, rows_of(0))
    project(2 * zm, rows_of(0))
    for d in range(2):
        near_copy(d, 1 - d, 0).start()
    project(2 * zp + 1 - yh, rows_of(1))
    g_cross(1)
    project(2 * zp, rows_of(0))
    project(2 * zm + 1, rows_of(0))
    for i in range(1, 3):
        project(2 * across[i] + yh, rows_of(1))
    project(2 * zm + 1 - yh, rows_of(1))
    project(2 * zf + yh, rows_of(1))
    project(2 * z, every)
    project(2 * z + 1, every)

    @pl.when(c > 0)
    def _():
        arrived(sex.at[pl.ds(0, 8)], halo_send.at[1], halo_recv.at[1])

    @pl.when(c == 0)
    def _():
        sex[0:8, :] = jnp.zeros((8, CHANS), F32)

    loads[4].wait()
    loads[5].wait()

    for r in range(Z_FIRST):
        for d in range(2):
            far_copy(d, r).wait_recv()
            block = 2 * ahead[d] + d
            pb[block, piece(r), :] = (
                pb[block, piece(r), :].astype(F32) + far[d, piece(r), :].astype(F32)
            ).astype(BF16)
            near_copy(d, d, r).start()
        for d in range(2):
            if r + 1 < Z_FIRST:
                near_copy(d, 1 - d, r + 1).start()
            if r + 2 < Z_FIRST:
                far_copy(d, r + 2).start()
        g_cross(2)
        g_cross(3)
        if r == 0:
            lax.fori_loop(0, 8, short_block, 0)
        for j in range(Y_FIRST):
            g_merge(0, j)
            for d in range(2):
                gfar_copy(d, j).start()
        @pl.when(c > 0)
        def _():
            arrived(mrx.at[pl.ds(0, TAPS)], halo_send.at[0], halo_recv.at[0])

        @pl.when(c == 0)
        def _():
            mrx[0:TAPS, :] = jnp.zeros((TAPS, CHANS), BF16)
        lax.fori_loop(0, 8, medium_block, 0)
    for i in range(2):
        for j in range(Y_FIRST):
            g_merge(i + 1, j)
            gnear_copy(i, 0, j).start()
    for j in range(Y_FIRST):
        for d in range(2):
            gfar_copy(d, j).wait_recv()
            block = 2 * ahead[d] + yh
            pb[block, g_half(j, d), :] = (
                pb[block, g_half(j, d), :].astype(F32) + gfar[d, j].astype(F32)
            ).astype(BF16)
            gnear_copy(d, 1, j).start()
    finish(Z_FIRST - 1)
    for j in range(Y_FIRST):
        g_merge(3, j)
    for r in range(Z_FIRST):
        side_copy(r).wait_recv()
        attn_out[piece(r), :] = (
            acc_own[piece(r), :] + yb[piece(r), :].astype(F32)
        ).astype(BF16)
    for j in range(Y_FIRST):
        for d in range(2):
            for merged in range(2):
                gnear_copy(d, merged, j).wait_recv()
        for h in range(2):
            attn_out[g_half(j, h), :] = (
                pb[2 * z + yh, g_half(j, h), :].astype(F32)
                + gnear[0, 1 - h, j].astype(F32)
                + gnear[1, h, j].astype(F32)
            ).astype(BF16)

    @pl.when(c < 15)
    def _():
        se_halo.wait_send()
        mr_halo.wait_send()

    for i, flip in enumerate(FLIPS):
        dest = flipped(flip)
        kv_copy(i, dest, 0).wait_send()
        kv_copy(i, dest, 1).wait_send()
        q_copy(i, dest).wait_send()

    @pl.when(jnp.logical_not(even))
    def _():
        sib_q.wait_send()

    def forwarded(i, _):
        forward(i).wait_send()
        stays = jnp.logical_and(i == chip, even)

        @pl.when(jnp.logical_not(stays))
        def _():
            head_copy(i, 1).wait_send()

        return 0

    lax.fori_loop(0, 8, forwarded, 0)
    for d in range(2):
        for r in range(Z_FIRST):
            far_copy(d, r).wait_send()
            for h in range(2):
                near_copy(d, h, r).wait_send()
        for j in range(Y_FIRST):
            gfar_copy(d, j).wait_send()
            for merged in range(2):
                gnear_copy(d, merged, j).wait_send()
    for r in range(Z_FIRST):
        side_copy(r).wait_send()
    for j in range(Y_FIRST):
        for i in range(4):
            gy_copy(i, j).wait_send()


def local(*args):
    (sq, sk, sv, sf, ss, mq, mk, mv, mf, md, ms, q, k, v, w) = args
    any_spec = pl.BlockSpec(memory_space=pl.ANY)
    vmem = pl.BlockSpec(memory_space=pltpu.VMEM)
    out = jax.ShapeDtypeStruct((ROWS, CHANS), BF16)
    dma = pltpu.SemaphoreType.DMA
    outs = pl.pallas_call(
        kernel,
        name="mixers",
        out_shape=(pltpu.VMEM((ROWS, CHANS), BF16),) * 3,
        in_specs=[any_spec] * 15,
        out_specs=(vmem,) * 3,
        scratch_shapes=[
            pltpu.VMEM((6, ROWS, CHANS), BF16),
            pltpu.VMEM((SHORT, 64), F32),
            pltpu.VMEM((1, CHANS), F32),
            pltpu.VMEM((64, TAPS), F32),
            pltpu.VMEM((1, 64), F32),
            pltpu.VMEM((1, CHANS), F32),
            pltpu.VMEM((8 + ROWS, CHANS), F32),
            pltpu.VMEM((8, CHANS), F32),
            pltpu.VMEM((TAPS + ROWS, CHANS), BF16),
            pltpu.VMEM((64, TAPS), F32),
            pltpu.VMEM((8, 2, 2 * ROWS, HEAD), BF16),
            pltpu.VMEM((8, ROWS, HEAD), BF16),
            pltpu.VMEM((8, ROWS, HEAD), BF16),
            pltpu.VMEM((ROWS, CHANS), BF16),
            pltpu.VMEM((8, CHANS, CHANS), BF16),
            pltpu.VMEM((8, ROWS, CHANS), BF16),
            pltpu.VMEM((8, ROWS, HEAD), F32),
            pltpu.VMEM((8, ROWS, HEAD), F32),
            pltpu.VMEM((8, ROWS, HEAD), F32),
            pltpu.VMEM((ROWS, 2 * ROWS), F32),
            pltpu.VMEM((ROWS, 2 * ROWS), F32),
            pltpu.VMEM((2, F_ROWS, CHANS), BF16),
            pltpu.VMEM((2, 2, F_ROWS, CHANS), BF16),
            pltpu.VMEM((F_ROWS, CHANS), BF16),
            pltpu.VMEM((F_ROWS, CHANS), BF16),
            pltpu.VMEM((F_ROWS, CHANS), F32),
            pltpu.VMEM((4, G_ROWS, CHANS), BF16),
            pltpu.VMEM((2, Y_FIRST, HALF, CHANS), BF16),
            pltpu.VMEM((2, 2, Y_FIRST, HALF, CHANS), BF16),
            dma((6,)), dma((5,)), dma((8,)),
            dma((2,)), dma((2,)),
            dma((7, 2)), dma((8, 2)), dma((8,)), dma((8,)),
            dma((8,)), dma((8,)), dma((8, 2)), dma((8, 2)),
            dma((2, Z_FIRST)), dma((2, Z_FIRST)),
            dma((2, 2, Z_FIRST)), dma((2, 2, Z_FIRST)),
            dma((Z_FIRST,)), dma((Z_FIRST,)),
            dma((4, Y_FIRST)), dma((4, Y_FIRST)),
            dma((2, Y_FIRST)), dma((2, Y_FIRST)),
            dma((2, 2, Y_FIRST)), dma((2, 2, Y_FIRST)),
        ],
        compiler_params=pltpu.CompilerParams(
            collective_id=0, has_side_effects=True, vmem_limit_bytes=56 * 1024 * 1024
        ),
        cost_estimate=pl.CostEstimate(
            flops=12 * 10**9, bytes_accessed=28 * 2**20, transcendentals=5 * 10**6
        ),
    )(
        sq, sk, sv, sf.T, ss.reshape(1, CHANS), mq, mk, mv, mf, md.reshape(1, 64),
        ms.reshape(1, CHANS), q, k, v, w,
    )
    return outs


def solution(mesh):
    block = P("ctx", "tp")
    in_specs = (
        block, block, block, P("tp", None), P("tp"),
        block, block, block, P("tp", None), P("tp"), P("tp"),
        block, block, block, P("tp", None),
    )
    return jax.shard_map(
        local, mesh=mesh, in_specs=in_specs, out_specs=(block, block, block), check_vma=False
    )
```

```python
import functools
import math

import jax
import jax.numpy as jnp
from jax import lax
from jax.experimental import pallas as pl
from jax.experimental.pallas import tpu as pltpu
from jax.sharding import PartitionSpec as P

F32 = jnp.float32
BF16 = jnp.bfloat16
HEAD = 128
ROWS = 256
CHANS = 1024
TAPS = 128
SHORT = 7
PIECE = 128
HALF = PIECE // 2
Z_FIRST = 1
Y_FIRST = ROWS // PIECE - Z_FIRST
F_ROWS = Z_FIRST * PIECE
G_ROWS = Y_FIRST * PIECE
EXP_SCALE = HEAD ** (-0.5) * math.log2(math.e)
FLIPS = (7, 1, 6, 2, 5, 3, 4)


def kernel(
    sq, sk, sv, sf_in, ss_in, mq, mk, mv, mf_in, md_in, ms_in, q, k, v, w,
    se_out, mr_out, attn_out,
    ld, sf, ss, mf, md, ms, sex, fexp, mrx, rtap, kv, qb, ob, hb, wb, pb, tops, norms, mixes, score_a, score_b,
    far, near, fin, yb, acc_own, gy, gfar, gnear,
    ld_sem, small_sem, w_sem,
    halo_send, halo_recv,
    kv_send, kv_recv, fwd_send, fwd_recv, q_send, q_recv, h_send, h_recv,
    far_send, far_recv, near_send, near_recv, y_send, y_recv,
    gy_send, gy_recv, gfar_send, gfar_recv, gnear_send, gnear_recv,
):
    c = lax.axis_index("ctx")
    t = lax.axis_index("tp")
    core = lax.rem(c, 2)
    chip = c // 2
    px = lax.rem(chip, 4)
    py = chip // 4
    sib = c + 1 - 2 * core
    z = t // 2
    yh = lax.rem(t, 2)
    zp = lax.rem(z + 1, 4)
    zm = lax.rem(z + 3, 4)
    zf = lax.rem(z + 2, 4)
    up = 2 * zp + yh
    down = 2 * zm + yh
    side = 2 * z + 1 - yh

    def remote(src, dst, send, recv, **where):
        return pltpu.make_async_remote_copy(
            src_ref=src, dst_ref=dst, send_sem=send, recv_sem=recv,
            device_id=where, device_id_type=pl.DeviceIdType.MESH,
        )

    def arrived(dst, send, recv):
        remote(dst, dst, send, recv, ctx=sib).wait_recv()

    barrier = pltpu.get_barrier_semaphore()

    def greet(i, _):
        pl.semaphore_signal(
            barrier, inc=1, device_id={"ctx": lax.rem(c + i, 16)},
            device_id_type=pl.DeviceIdType.MESH,
        )
        return 0

    lax.fori_loop(1, 16, greet, 0)
    for peer in (up, down, side):
        pl.semaphore_signal(
            barrier, inc=1, device_id={"tp": peer}, device_id_type=pl.DeviceIdType.MESH
        )

    loads = [
        pltpu.make_async_copy(src, ld.at[i], ld_sem.at[i])
        for i, src in enumerate((mk, mv, sk, sv, sq, mq))
    ]
    for copy in loads:
        copy.start()

    pl.semaphore_wait(barrier, 18)

    own_rows = pl.ds(pl.multiple_of(core * ROWS, ROWS), ROWS)
    q_core = lax.rem(core + chip, 2)

    def head_cols(h):
        return pl.ds(pl.multiple_of(h * HEAD, HEAD), HEAD)

    def flipped(flip):
        bits = (lax.rem(px, 2), px // 2, py)
        out = 0
        for i, bit in enumerate(bits):
            m = flip // 2**i % 2
            out = out + 2**i * (bit + m - 2 * bit * m)
        return out

    def kv_copy(i, dest, part):
        return remote(
            (k, v)[part].at[:, head_cols(dest)], kv.at[chip, part, own_rows],
            kv_send.at[i, part], kv_recv.at[chip, part], ctx=2 * dest + core,
        )

    def q_copy(i, dest):
        return remote(
            q.at[:, head_cols(dest)], qb.at[chip],
            q_send.at[i], q_recv.at[chip], ctx=2 * dest + q_core,
        )

    def send_kv(first, last):
        for i in range(first, last):
            kv_copy(i, flipped(FLIPS[i]), 0).start()
            kv_copy(i, flipped(FLIPS[i]), 1).start()

    for i, flip in enumerate(FLIPS):
        q_copy(i, flipped(flip)).start()
    send_kv(0, 3)
    own_kv = [
        pltpu.make_async_copy(
            src.at[:, head_cols(chip)], kv.at[chip, part, own_rows], kv_recv.at[chip, part]
        )
        for part, src in enumerate((k, v))
    ]
    for copy in own_kv:
        copy.start()
    own_q = pltpu.make_async_copy(q.at[:, head_cols(chip)], qb.at[chip], q_recv.at[chip])
    sib_q = remote(
        q.at[:, head_cols(chip)], qb.at[chip], q_send.at[7], q_recv.at[chip], ctx=sib
    )
    even = lax.rem(chip, 2) == 0

    @pl.when(even)
    def _():
        own_q.start()

    @pl.when(jnp.logical_not(even))
    def _():
        sib_q.start()

    small = [
        pltpu.make_async_copy(src, dst, small_sem.at[i])
        for i, (src, dst) in enumerate(
            ((sf_in, sf), (ss_in, ss), (mf_in, mf), (md_in, md), (ms_in, ms))
        )
    ]
    for copy in small:
        copy.start()

    def product(first, second, r):
        rows = pl.ds(pl.multiple_of(r * 32, 32), 32)
        return (ld[first, rows, :].astype(F32) * ld[second, rows, :].astype(F32)).astype(BF16)

    loads[0].wait()
    loads[1].wait()

    def mr_product(r, _):
        mrx[pl.ds(pl.multiple_of(TAPS + r * 32, 32), 32), :] = product(0, 1, r)
        return 0

    lax.fori_loop(0, ROWS // 32, mr_product, 0)
    loads[2].wait()
    loads[3].wait()

    def se_product(r, _):
        sex[pl.ds(pl.multiple_of(8 + r * 32, 8), 32), :] = product(2, 3, r).astype(F32)
        return 0

    lax.fori_loop(0, ROWS // 32, se_product, 0)

    mr_halo = remote(
        mrx.at[pl.ds(ROWS, TAPS)], mrx.at[pl.ds(0, TAPS)],
        halo_send.at[0], halo_recv.at[0], ctx=lax.rem(c + 1, 16),
    )
    se_halo = remote(
        sex.at[pl.ds(ROWS, 8)], sex.at[pl.ds(0, 8)],
        halo_send.at[1], halo_recv.at[1], ctx=lax.rem(c + 1, 16),
    )

    weights = [
        pltpu.make_async_copy(w.at[:, pl.ds(i * CHANS, CHANS)], wb.at[i], w_sem.at[i])
        for i in range(8)
    ]
    for copy in weights:
        copy.start()

    for copy in small:
        copy.wait()

    group_of = lax.broadcasted_iota(jnp.int32, (64, CHANS), 1) // 16
    mine = group_of == lax.broadcasted_iota(jnp.int32, (64, CHANS), 0)
    row64 = lax.broadcasted_iota(jnp.int32, (64, 64), 0)
    lane64 = lax.broadcasted_iota(jnp.int32, (64, 64), 1)

    def as_column(row):
        return jnp.sum(jnp.where(row64 == lane64, row, 0.0), axis=1, keepdims=True)

    for j in range(SHORT):
        fexp[j : j + 1, :] = jnp.sum(
            jnp.where(mine, as_column(sf[j : j + 1, :]), 0.0), axis=0, keepdims=True
        )

    def short_block(l, _):
        cols = pl.ds(pl.multiple_of(l * 128, 128), 128)
        conv = sex[8 : 8 + ROWS, cols] * fexp[0:1, cols]
        for j in range(1, SHORT):
            conv = conv + sex[8 - j : 8 - j + ROWS, cols] * fexp[j : j + 1, cols]
        skipped = ss[0:1, cols] * sex[8 : 8 + ROWS, cols]
        se_out[:, cols] = (ld[4, :, cols].astype(F32) * (conv + skipped)).astype(BF16)
        return 0

    decay = as_column(md[...])
    tap_index = lax.broadcasted_iota(jnp.int32, (64, TAPS), 1).astype(F32)
    taps = (mf[...] * jnp.exp(-decay * tap_index)).astype(BF16)
    r128 = lax.broadcasted_iota(jnp.int32, (TAPS, TAPS), 0)
    l128 = lax.broadcasted_iota(jnp.int32, (TAPS, TAPS), 1)
    flip = jnp.where(lax.rem(r128 + l128, TAPS) == 0, 1.0, 0.0).astype(BF16)
    rtap[...] = jnp.dot(taps, flip, preferred_element_type=F32)

    later = l128 > r128
    lane_group = lax.rem(lax.broadcasted_iota(jnp.int32, (TAPS, 2 * TAPS), 1), TAPS) // 16

    def medium_block(l, _):
        cols = pl.ds(pl.multiple_of(l * 128, 128), 128)
        window = jnp.concatenate(
            [mrx[0 : 2 * TAPS, cols], mrx[TAPS : 3 * TAPS, cols]], axis=1
        )
        block_taps = rtap[pl.ds(pl.multiple_of(l * 8, 8), 8), :]
        conv = jnp.zeros((TAPS, 2 * TAPS), F32)
        for g in range(8):
            row = jnp.broadcast_to(block_taps[g : g + 1, :], (TAPS, TAPS))
            turned = pltpu.roll(row, 0, 1, stride=1, stride_axis=0)
            table = jnp.concatenate(
                [jnp.where(later, turned, 0.0), jnp.where(later, 0.0, turned)], axis=1
            ).astype(BF16)
            conv = jnp.where(
                lane_group == g, jnp.dot(table, window, preferred_element_type=F32), conv
            )
        for b in range(2):
            rows = pl.ds(b * TAPS, TAPS)
            source = mrx[TAPS + b * TAPS : 2 * TAPS + b * TAPS, cols].astype(F32)
            total = conv[:, b * TAPS : (b + 1) * TAPS] + ms[0:1, cols] * source
            mr_out[rows, cols] = (ld[5, rows, cols].astype(F32) * total).astype(BF16)
        return 0

    def forward(src_chip):
        piece = kv.at[src_chip, :, own_rows]
        return remote(
            piece, piece, fwd_send.at[src_chip], fwd_recv.at[src_chip], ctx=sib
        )

    sib_rows = pl.ds(pl.multiple_of((1 - core) * ROWS, ROWS), ROWS)

    def take(src_chip):
        for part in range(2):
            arrived(
                kv.at[src_chip, part, own_rows], fwd_send.at[src_chip], kv_recv.at[src_chip, part]
            )
        forward(src_chip).start()

    def query_here(i, _):
        tops[i] = jnp.full((ROWS, HEAD), -1e30, F32)
        norms[i] = jnp.zeros((ROWS, HEAD), F32)
        mixes[i] = jnp.zeros((ROWS, HEAD), F32)
        arrived(qb.at[i], q_send.at[0], q_recv.at[i])
        return 0

    lax.fori_loop(0, 8, query_here, 0)
    send_kv(3, 5)

    q_row = lax.broadcasted_iota(jnp.int32, (ROWS, 2 * ROWS), 0)
    k_row = lax.broadcasted_iota(jnp.int32, (ROWS, 2 * ROWS), 1)

    def weigh(scores, chunk, slot, masked):
        s = scores[...]
        if masked:
            limit = jnp.where(slot == chunk, lax.rem(core + slot, 2) * ROWS, 2 * ROWS)
            s = jnp.where(k_row <= q_row + limit, s, -1e30)
        old = tops[slot]
        new = jnp.maximum(old, jnp.max(s, axis=1, keepdims=True))
        factor = jnp.exp2((old - new) * EXP_SCALE)
        expo = jnp.exp2((s - jnp.concatenate([new] * 4, axis=1)) * EXP_SCALE)
        mixed = jnp.dot(expo.astype(BF16), kv[chunk, 1], preferred_element_type=F32)
        tops[slot] = new
        norms[slot] = norms[slot] * factor + (
            expo[:, 0:128] + expo[:, 128:256] + expo[:, 256:384] + expo[:, 384:512]
        )
        mixes[slot] = mixes[slot] * factor + mixed

    def wave(m, _):
        first = flipped(m)
        low = jnp.minimum(first, 7 - first)
        high = 7 - low
        take(first)
        take(7 - first)

        @pl.when(m == 0)
        def _():
            send_kv(5, 7)

        for src_chip in (first, 7 - first):
            arrived(kv.at[src_chip, :, sib_rows], fwd_send.at[src_chip], fwd_recv.at[src_chip])

        def step(j):
            of_low = j < 8 - low
            return jnp.where(of_low, low, high), jnp.where(of_low, low + j, j - 1)

        def score(j):
            chunk, slot = step(j)
            (score_a, score_b)[j % 2][...] = lax.dot_general(
                qb[slot], kv[chunk, 0], (((1,), (1,)), ((), ())), preferred_element_type=F32
            )

        score(0)
        for j in range(9):
            if j < 8:
                score(j + 1)
            weigh((score_a, score_b)[j % 2], *step(j), j == 0 or j > 4)
        return 0

    lax.fori_loop(0, 4, wave, 0)

    def rows_of(half):
        return pl.ds(half * F_ROWS, F_ROWS if half == 0 else G_ROWS)

    def head_copy(slot, half):
        return remote(
            ob.at[slot, rows_of(half)], hb.at[rows_of(half), head_cols(chip)],
            h_send.at[slot, half], h_recv.at[chip, half],
            ctx=2 * slot + lax.rem(core + slot, 2),
        )

    def give_back(slot, half):
        stays = jnp.logical_and(slot == chip, even)

        @pl.when(stays)
        def _():
            pltpu.make_async_copy(
                ob.at[slot, rows_of(half)], hb.at[rows_of(half), head_cols(chip)],
                h_recv.at[chip, half],
            ).start()

        @pl.when(jnp.logical_not(stays))
        def _():
            head_copy(slot, half).start()

    def complete(half):
        def one(o, _):
            slot = lax.rem(chip + 1 + o, 8)
            rows = rows_of(half)
            ob[slot, rows, :] = (
                mixes[slot, rows, :] / jnp.sum(norms[slot, rows, :], axis=1, keepdims=True)
            ).astype(BF16)
            if half == 0:
                give_back(slot, half)
            return 0

        lax.fori_loop(0, 8, one, 0)

    def heads_here(half):
        def one(i, _):
            arrived(hb.at[rows_of(half), head_cols(i)], h_send.at[0, half], h_recv.at[i, half])
            return 0

        lax.fori_loop(0, 8, one, 0)

    complete(0)
    complete(1)

    def second_half(o, _):
        slot = lax.rem(chip + 1 + o, 8)

        @pl.when(jnp.logical_not(jnp.logical_and(slot == chip, even)))
        def _():
            head_copy(slot, 0).wait_send()

        give_back(slot, 1)
        return 0

    lax.fori_loop(0, 8, second_half, 0)

    @pl.when(c < 15)
    def _():
        se_halo.start()
        mr_halo.start()

    for copy in weights:
        copy.wait()
    heads_here(0)

    every = pl.ds(0, ROWS)

    def project(block, rows):
        def columns(n, _):
            cols = pl.ds(pl.multiple_of(n * 256, 256), 256)
            pb[block, rows, cols] = jnp.dot(
                hb[rows, :], wb[block, :, cols], preferred_element_type=F32
            ).astype(BF16)
            return 0

        lax.fori_loop(0, CHANS // 256, columns, 0)

    def piece(r):
        return pl.ds(r * PIECE, PIECE)

    ahead = (zp, zm)
    to = (up, down)

    def far_copy(d, r):
        return remote(
            pb.at[2 * zf + d, piece(r)], far.at[d, piece(r)],
            far_send.at[d, r], far_recv.at[d, r], tp=to[d],
        )

    def near_copy(d, h, r):
        return remote(
            pb.at[2 * ahead[d] + h, piece(r)], near.at[d, h, piece(r)],
            near_send.at[d, h, r], near_recv.at[d, h, r], tp=to[d],
        )

    def side_copy(r):
        return remote(
            fin.at[piece(r)], yb.at[piece(r)], y_send.at[r], y_recv.at[r], tp=side
        )

    def finish(r):
        for d in range(2):
            for h in range(2):
                near_copy(d, h, r).wait_recv()

        def total(h):
            return (
                pb[2 * z + h, piece(r), :].astype(F32)
                + near[0, h, piece(r), :].astype(F32)
                + near[1, h, piece(r), :].astype(F32)
            )

        fin[piece(r), :] = total(1 - yh).astype(BF16)
        side_copy(r).start()
        acc_own[piece(r), :] = total(yh)

    across = (zf, zp, zm, z)

    def g_piece(j):
        return pl.ds(F_ROWS + j * PIECE, PIECE)

    def g_half(j, h):
        return pl.ds(F_ROWS + j * PIECE + h * HALF, HALF)

    def gy_copy(i, j):
        return remote(
            pb.at[2 * across[i] + 1 - yh, g_piece(j)], gy.at[i, pl.ds(j * PIECE, PIECE)],
            gy_send.at[i, j], gy_recv.at[i, j], tp=side,
        )

    def gfar_copy(d, j):
        return remote(
            pb.at[2 * zf + yh, g_half(j, d)], gfar.at[d, j],
            gfar_send.at[d, j], gfar_recv.at[d, j], tp=to[d],
        )

    def gnear_copy(d, merged, j):
        return remote(
            pb.at[2 * ahead[d] + yh, g_half(j, d if merged else 1 - d)], gnear.at[d, merged, j],
            gnear_send.at[d, merged, j], gnear_recv.at[d, merged, j], tp=to[d],
        )

    def g_cross(i):
        for j in range(Y_FIRST):
            gy_copy(i, j).start()

    def g_merge(i, j):
        gy_copy(i, j).wait_recv()
        block = 2 * across[i] + yh
        pb[block, g_piece(j), :] = (
            pb[block, g_piece(j), :].astype(F32)
            + gy[i, pl.ds(j * PIECE, PIECE), :].astype(F32)
        ).astype(BF16)

    for h in range(2):
        project(2 * zf + h, rows_of(0))
    for r in range(1):
        for d in range(2):
            far_copy(d, r).start()
    heads_here(1)
    project(2 * zf + 1 - yh, rows_of(1))
    g_cross(0)
    project(2 * zp + 1, rows_of(0))
    project(2 * zm, rows_of(0))
    for d in range(2):
        near_copy(d, 1 - d, 0).start()
    project(2 * zp + 1 - yh, rows_of(1))
    g_cross(1)
    project(2 * zp, rows_of(0))
    project(2 * zm + 1, rows_of(0))
    for i in range(1, 3):
        project(2 * across[i] + yh, rows_of(1))
    project(2 * zm + 1 - yh, rows_of(1))
    project(2 * zf + yh, rows_of(1))
    project(2 * z, every)
    project(2 * z + 1, every)

    @pl.when(c > 0)
    def _():
        arrived(sex.at[pl.ds(0, 8)], halo_send.at[1], halo_recv.at[1])

    @pl.when(c == 0)
    def _():
        sex[0:8, :] = jnp.zeros((8, CHANS), F32)

    loads[4].wait()
    loads[5].wait()

    for r in range(Z_FIRST):
        for d in range(2):
            far_copy(d, r).wait_recv()
            block = 2 * ahead[d] + d
            pb[block, piece(r), :] = (
                pb[block, piece(r), :].astype(F32) + far[d, piece(r), :].astype(F32)
            ).astype(BF16)
            near_copy(d, d, r).start()
        for d in range(2):
            if r + 1 < Z_FIRST:
                near_copy(d, 1 - d, r + 1).start()
            if r + 2 < Z_FIRST:
                far_copy(d, r + 2).start()
        g_cross(2)
        g_cross(3)
        if r == 0:
            lax.fori_loop(0, 8, short_block, 0)
        for j in range(Y_FIRST):
            g_merge(0, j)
            for d in range(2):
                gfar_copy(d, j).start()
        @pl.when(c > 0)
        def _():
            arrived(mrx.at[pl.ds(0, TAPS)], halo_send.at[0], halo_recv.at[0])

        @pl.when(c == 0)
        def _():
            mrx[0:TAPS, :] = jnp.zeros((TAPS, CHANS), BF16)
        lax.fori_loop(0, 8, medium_block, 0)
    finish(Z_FIRST - 1)
    for i in range(2):
        for j in range(Y_FIRST):
            g_merge(i + 1, j)
            gnear_copy(i, 0, j).start()
    for j in range(Y_FIRST):
        for d in range(2):
            gfar_copy(d, j).wait_recv()
            block = 2 * ahead[d] + yh
            pb[block, g_half(j, d), :] = (
                pb[block, g_half(j, d), :].astype(F32) + gfar[d, j].astype(F32)
            ).astype(BF16)
            gnear_copy(d, 1, j).start()
    for j in range(Y_FIRST):
        g_merge(3, j)
    for r in range(Z_FIRST):
        side_copy(r).wait_recv()
        attn_out[piece(r), :] = (
            acc_own[piece(r), :] + yb[piece(r), :].astype(F32)
        ).astype(BF16)
    for j in range(Y_FIRST):
        for d in range(2):
            for merged in range(2):
                gnear_copy(d, merged, j).wait_recv()
        for h in range(2):
            attn_out[g_half(j, h), :] = (
                pb[2 * z + yh, g_half(j, h), :].astype(F32)
                + gnear[0, 1 - h, j].astype(F32)
                + gnear[1, h, j].astype(F32)
            ).astype(BF16)

    @pl.when(c < 15)
    def _():
        se_halo.wait_send()
        mr_halo.wait_send()

    for i, flip in enumerate(FLIPS):
        dest = flipped(flip)
        kv_copy(i, dest, 0).wait_send()
        kv_copy(i, dest, 1).wait_send()
        q_copy(i, dest).wait_send()

    @pl.when(jnp.logical_not(even))
    def _():
        sib_q.wait_send()

    def forwarded(i, _):
        forward(i).wait_send()
        stays = jnp.logical_and(i == chip, even)

        @pl.when(jnp.logical_not(stays))
        def _():
            head_copy(i, 1).wait_send()

        return 0

    lax.fori_loop(0, 8, forwarded, 0)
    for d in range(2):
        for r in range(Z_FIRST):
            far_copy(d, r).wait_send()
            for h in range(2):
                near_copy(d, h, r).wait_send()
        for j in range(Y_FIRST):
            gfar_copy(d, j).wait_send()
            for merged in range(2):
                gnear_copy(d, merged, j).wait_send()
    for r in range(Z_FIRST):
        side_copy(r).wait_send()
    for j in range(Y_FIRST):
        for i in range(4):
            gy_copy(i, j).wait_send()


def local(*args):
    (sq, sk, sv, sf, ss, mq, mk, mv, mf, md, ms, q, k, v, w) = args
    any_spec = pl.BlockSpec(memory_space=pl.ANY)
    vmem = pl.BlockSpec(memory_space=pltpu.VMEM)
    out = jax.ShapeDtypeStruct((ROWS, CHANS), BF16)
    dma = pltpu.SemaphoreType.DMA
    outs = pl.pallas_call(
        kernel,
        name="mixers",
        out_shape=(pltpu.VMEM((ROWS, CHANS), BF16),) * 3,
        in_specs=[any_spec] * 15,
        out_specs=(vmem,) * 3,
        scratch_shapes=[
            pltpu.VMEM((6, ROWS, CHANS), BF16),
            pltpu.VMEM((SHORT, 64), F32),
            pltpu.VMEM((1, CHANS), F32),
            pltpu.VMEM((64, TAPS), F32),
            pltpu.VMEM((1, 64), F32),
            pltpu.VMEM((1, CHANS), F32),
            pltpu.VMEM((8 + ROWS, CHANS), F32),
            pltpu.VMEM((8, CHANS), F32),
            pltpu.VMEM((TAPS + ROWS, CHANS), BF16),
            pltpu.VMEM((64, TAPS), F32),
            pltpu.VMEM((8, 2, 2 * ROWS, HEAD), BF16),
            pltpu.VMEM((8, ROWS, HEAD), BF16),
            pltpu.VMEM((8, ROWS, HEAD), BF16),
            pltpu.VMEM((ROWS, CHANS), BF16),
            pltpu.VMEM((8, CHANS, CHANS), BF16),
            pltpu.VMEM((8, ROWS, CHANS), BF16),
            pltpu.VMEM((8, ROWS, HEAD), F32),
            pltpu.VMEM((8, ROWS, HEAD), F32),
            pltpu.VMEM((8, ROWS, HEAD), F32),
            pltpu.VMEM((ROWS, 2 * ROWS), F32),
            pltpu.VMEM((ROWS, 2 * ROWS), F32),
            pltpu.VMEM((2, F_ROWS, CHANS), BF16),
            pltpu.VMEM((2, 2, F_ROWS, CHANS), BF16),
            pltpu.VMEM((F_ROWS, CHANS), BF16),
            pltpu.VMEM((F_ROWS, CHANS), BF16),
            pltpu.VMEM((F_ROWS, CHANS), F32),
            pltpu.VMEM((4, G_ROWS, CHANS), BF16),
            pltpu.VMEM((2, Y_FIRST, HALF, CHANS), BF16),
            pltpu.VMEM((2, 2, Y_FIRST, HALF, CHANS), BF16),
            dma((6,)), dma((5,)), dma((8,)),
            dma((2,)), dma((2,)),
            dma((7, 2)), dma((8, 2)), dma((8,)), dma((8,)),
            dma((8,)), dma((8,)), dma((8, 2)), dma((8, 2)),
            dma((2, Z_FIRST)), dma((2, Z_FIRST)),
            dma((2, 2, Z_FIRST)), dma((2, 2, Z_FIRST)),
            dma((Z_FIRST,)), dma((Z_FIRST,)),
            dma((4, Y_FIRST)), dma((4, Y_FIRST)),
            dma((2, Y_FIRST)), dma((2, Y_FIRST)),
            dma((2, 2, Y_FIRST)), dma((2, 2, Y_FIRST)),
        ],
        compiler_params=pltpu.CompilerParams(
            collective_id=0, has_side_effects=True, vmem_limit_bytes=56 * 1024 * 1024
        ),
        cost_estimate=pl.CostEstimate(
            flops=12 * 10**9, bytes_accessed=28 * 2**20, transcendentals=5 * 10**6
        ),
    )(
        sq, sk, sv, sf.T, ss.reshape(1, CHANS), mq, mk, mv, mf, md.reshape(1, 64),
        ms.reshape(1, CHANS), q, k, v, w,
    )
    return outs


def solution(mesh):
    block = P("ctx", "tp")
    in_specs = (
        block, block, block, P("tp", None), P("tp"),
        block, block, block, P("tp", None), P("tp"), P("tp"),
        block, block, block, P("tp", None),
    )
    return jax.shard_map(
        local, mesh=mesh, in_specs=in_specs, out_specs=(block, block, block), check_vma=False
    )
```
